32 devices in a mesh: px: 4 (over y, x), py: 4 (over z), pz: 2 (over core).
Axes of the slice: x: 2, y: 2, z: 4, core: 2. Of those that a mesh axis runs over, the one named last changes fastest.
Arguments:
- rhs: float32 [32, 512, 512], P('pz', 'py', 'px'), may hold values from -4 to 6
- coeff: float32 [32, 512, 512], P('pz', 'py', 'px'), may hold values from 0.1 to 10
- shift: float32 [32, 512, 512], P('pz', 'py', 'px'), may hold values from 0.01 to 0.3
Outputs:
- solution: float32 [32, 512, 512], P('pz', 'py', 'px')
The draws below stay inside these ranges and needn't reach their ends.
All inputs are finite; a program needn't handle non-finite values.
Results may differ from the reference program's by a relative error of at most 0.0001.
Values sent between devices are 32-bit elements; how exact they have to be, the bound alone decides.
No kernel may reach another device: no remote copies, remote signals or barrier semaphores. Data moves between devices by JAX's collectives and lax.ppermute only.
A program may use at most 256 MiB of HBM per device.

```python
import math
import jax
import jax.numpy as jnp
from jax import lax

LEVELS = 3
DEG = 4
CDEG = 8
NZ = 32
NY = 512
NX = 512


def draw_coeff(key, part):
    block_key = jax.random.fold_in(key, 11)
    cell_key = jax.random.fold_in(key, 12)
    span = 2 ** LEVELS
    blocks = jnp.exp(jax.random.uniform(block_key, (NZ // span, NY // span, NX // span), jnp.float32, math.log(0.2), math.log(5.0)))
    blocks = jnp.repeat(jnp.repeat(jnp.repeat(blocks, span, axis=0), span, axis=1), span, axis=2)
    cells = jnp.exp(jax.random.uniform(cell_key, (NZ, NY, NX), jnp.float32, math.log(0.5), math.log(2.0)))
    return (blocks * cells).astype(jnp.float32)


def draw_rhs(key, part):
    rough_key = jax.random.fold_in(key, 21)
    rough = jnp.clip(jax.random.normal(rough_key, (NZ, NY, NX), jnp.float32), -3.5, 3.5)
    place_z = (jnp.arange(NZ, dtype=jnp.float32) + 0.5) / NZ
    place_y = (jnp.arange(NY, dtype=jnp.float32) + 0.5) / NY
    place_x = (jnp.arange(NX, dtype=jnp.float32) + 0.5) / NX
    wave = jnp.sin(2.0 * math.pi * (place_z[:, None, None] + place_y[None, :, None])) * jnp.cos(2.0 * math.pi * place_x[None, None, :])
    smooth_part = 1.0 + 0.5 * wave
    return (rough + smooth_part).astype(jnp.float32)


def level_of(stream_key, dims, split, low, high):
    level = 1.0
    for dim, blocks in split:
        draws = jax.random.uniform(jax.random.fold_in(jax.random.fold_in(stream_key, 6), dim), (blocks,), jnp.float32, low / len(split), high / len(split))
        level = level * jnp.repeat(jnp.exp(draws), dims[dim] // blocks).reshape((-1,) + (1,) * (len(dims) - 1 - dim))
    return level


def setup_inputs(seed: int = 0) -> dict:
    streams_of = jax.random.split(jax.random.key(seed), 4)
    return {
        "rhs": draw_rhs(jax.random.fold_in(streams_of[3], 71), 0),
        "coeff": draw_coeff(jax.random.fold_in(streams_of[3], 71), 0),
        "shift": jnp.clip(jnp.exp(math.log(0.3) - 3.4011974 * jax.random.uniform(streams_of[2], (NZ, NY, NX), jnp.float32) ** level_of(streams_of[2], (NZ, NY, NX), ((0, 2), (1, 4), (2, 4)), -0.2, 0.2)), 0.01, 0.3),
    }


lower_bound = 0.4
upper_bound = 2.0


def neighbour_views(shape):
    result = []
    for axis_index in range(3):
        for offset in (0, 2):
            index_list = [slice(1, 1 + shape[k]) for k in range(3)]
            index_list[axis_index] = slice(offset, offset + shape[axis_index])
            result.append(tuple(index_list))
    return result


def make_level(coeff_pad, shift_field, factor):
    center = coeff_pad[1:-1, 1:-1, 1:-1]
    weights = jnp.zeros_like(center)
    for view in neighbour_views(center.shape):
        weights = weights + 0.5 * (center + coeff_pad[view])
    inverse = 1.0 / (factor * weights + shift_field)
    return (coeff_pad, shift_field, factor, inverse)


def apply_operator(field_pad, level_data):
    coeff_pad, shift_field, factor, inverse = level_data
    center = field_pad[1:-1, 1:-1, 1:-1]
    coeff_center = coeff_pad[1:-1, 1:-1, 1:-1]
    total = jnp.zeros_like(center)
    for view in neighbour_views(center.shape):
        total = total + 0.5 * (coeff_center + coeff_pad[view]) * (center - field_pad[view])
    return factor * total + shift_field * center


def smooth(field, source, level_data, degree, padder):
    inverse = level_data[3]
    theta = 0.5 * (upper_bound + lower_bound)
    delta = 0.5 * (upper_bound - lower_bound)
    sigma = theta / delta
    rho_now = 1.0 / sigma
    if field is None:
        scaled = source * inverse
        update = scaled / theta
        field = update
    else:
        scaled = (source - apply_operator(padder(field), level_data)) * inverse
        update = scaled / theta
        field = field + update
    for sweep_index in range(degree - 1):
        scaled = (source - apply_operator(padder(field), level_data)) * inverse
        rho_next = 1.0 / (2.0 * sigma - rho_now)
        update = rho_next * rho_now * update + (2.0 * rho_next / delta) * scaled
        field = field + update
        rho_now = rho_next
    return field


def restrict(field):
    s0, s1, s2 = field.shape
    return field.reshape(s0 // 2, 2, s1 // 2, 2, s2 // 2, 2).mean(axis=(1, 3, 5))


def refine_axis(padded, axis_index):
    count = padded.shape[axis_index] - 2
    center = lax.slice_in_dim(padded, 1, count + 1, axis=axis_index)
    lower = lax.slice_in_dim(padded, 0, count, axis=axis_index)
    upper = lax.slice_in_dim(padded, 2, count + 2, axis=axis_index)
    even_part = 0.75 * center + 0.25 * lower
    odd_part = 0.75 * center + 0.25 * upper
    stacked = jnp.stack([even_part, odd_part], axis=axis_index + 1)
    shape = list(center.shape)
    shape[axis_index] = 2 * count
    return stacked.reshape(shape)


def prolong(padded):
    for axis_index in range(3):
        padded = refine_axis(padded, axis_index)
    return padded


def zero_pad(field):
    return jnp.pad(field, 1)


def reference(rhs, coeff, shift):
    levels_list = []
    coeff_now, shift_now = coeff, shift
    for depth in range(LEVELS):
        levels_list.append(make_level(zero_pad(coeff_now), shift_now, 0.25 ** depth))
        coeff_now = restrict(coeff_now)
        shift_now = restrict(shift_now)
    sources = [rhs]
    fields = []
    for depth in range(LEVELS):
        field = smooth(None, sources[depth], levels_list[depth], DEG, zero_pad)
        residual = sources[depth] - apply_operator(zero_pad(field), levels_list[depth])
        fields.append(field)
        sources.append(restrict(residual))
    coarse_level = make_level(zero_pad(coeff_now), shift_now, 0.25 ** LEVELS)
    coarse_field = smooth(None, sources[LEVELS], coarse_level, CDEG, zero_pad)
    padded = zero_pad(coarse_field)
    field = coarse_field
    for depth in range(LEVELS - 1, -1, -1):
        field = fields[depth] + prolong(padded)
        field = smooth(field, sources[depth], levels_list[depth], DEG, zero_pad)
        padded = zero_pad(field)
    return field
```

```python
import jax
import jax.numpy as jnp
from jax import lax
from jax.experimental import pallas as pl
from jax.experimental.pallas import tpu as pltpu
from jax.sharding import PartitionSpec as P

LEVELS = 3
DEG = 4
CDEG = 8
THETA = 1.2
DELTA = 0.8
F32 = jnp.float32
LANES = 128


def vmem(*shape):
    return pltpu.VMEM(shape, F32)


def shape(*dims):
    return jax.ShapeDtypeStruct(dims, F32)


def call(kernel, outs, scratch=(), ins=0, name=None):
    spec = pl.BlockSpec(memory_space=pltpu.VMEM)
    single = not isinstance(outs, (list, tuple))
    return pl.pallas_call(
        kernel,
        out_shape=outs,
        in_specs=[spec] * ins,
        out_specs=spec if single else [spec] * len(outs),
        scratch_shapes=list(scratch),
        compiler_params=pltpu.CompilerParams(vmem_limit_bytes=60 * 1024 * 1024),
        name=name,
    )


def dot(a, b):
    return jnp.dot(a, b, precision=lax.Precision.HIGHEST, preferred_element_type=F32)


def iota(rows, cols, axis):
    return lax.broadcasted_iota(jnp.int32, (rows, cols), axis)


def roll(value, amount):
    amount = amount % LANES
    return value if amount == 0 else pltpu.roll(value, amount, 1)


def chebyshev(degree):
    sigma = THETA / DELTA
    rho = 1.0 / sigma
    steps = [(0.0, 1.0 / THETA)]
    for _ in range(degree - 1):
        new = 1.0 / (2.0 * sigma - rho)
        steps.append((new * rho, 2.0 * new / DELTA))
        rho = new
    return steps


class Level:
    def __init__(self, refs, wrap):
        self.wx, self.wy, self.wz, self.f, self.dinv, self.u, self.v, self.d = refs
        self.tiles = self.u.shape[2] // LANES
        self.wrap = wrap

    def get(self, ref, z, row):
        return [ref[z, row : row + 8, LANES * t : LANES * (t + 1)] for t in range(self.tiles)]

    def put(self, ref, z, row, values):
        for t, value in enumerate(values):
            ref[z, row : row + 8, LANES * t : LANES * (t + 1)] = value

    def right(self, values):
        lane = iota(8, LANES, 1)
        rolled = [roll(v, -1) for v in values]
        if self.tiles == 1:
            return rolled
        return [jnp.where(lane == LANES - 1, rolled[1 - t], rolled[t]) for t in range(2)]

    def left(self, values):
        lane = iota(8, LANES, 1)
        rolled = [roll(v, 1) for v in values]
        if self.tiles == 1:
            return rolled
        return [jnp.where(lane == 0, rolled[1 - t], rolled[t]) for t in range(2)]


def each(fn, *lists):
    return [fn(*items) for items in zip(*lists)]


def setup(level, kappa, planes, first, last, coef):
    lane = iota(8, LANES, 1)
    half = 0.5 * kappa

    def zface(z, row):
        return each(lambda a, b: half * (a + b), level.get(coef, z, row), level.get(coef, z + 1, row))

    for t in range(first, last):
        level.put(level.wz, 0, 8 * t, zface(0, 8 * t))

    for row in (8 * first - 8,):
        def edge(z, carry):
            a = level.get(coef, z, row)
            b = level.get(coef, z, row + 1)
            level.put(level.wy, z, row, each(lambda p, q: half * (p + q), a, b))
            return carry
        lax.fori_loop(1, planes + 1, edge, 0)

    def body(z, carry):
        for t in range(first, last):
            row = 8 * t
            a = level.get(coef, z, row)
            ar = level.right(a)
            if level.wrap:
                ar = each(lambda v: jnp.where(lane == LANES - 1, 0.0, v), ar)
            wx = each(lambda p, q: half * (p + q), a, ar)
            wl = level.left(wx)
            if level.wrap:
                wl = each(lambda v, p: jnp.where(lane == 0, half * p, v), wl, a)
            wy = each(lambda p, q: half * (p + q), a, level.get(coef, z, row + 1))
            wd = each(lambda p, q: half * (p + q), a, level.get(coef, z, row - 1))
            wz = zface(z, row)
            wb = level.get(level.wz, z - 1, row)
            c = level.get(level.dinv, z, row)
            den = each(lambda p, q, r, s, t_, u_, v_: p + q + r + s + t_ + u_ + v_, wx, wl, wy, wd, wz, wb, c)
            inside = each(lambda v: v > 0.0, c)
            dinv = each(lambda m, v: jnp.where(m, 1.0 / jnp.where(m, v, 1.0), 0.0), inside, den)
            f = each(lambda v, w: v * w, level.get(level.f, z, row), dinv)
            if level.wrap:
                wx = each(lambda v: jnp.where(lane == LANES - 1, 0.0, v), wx)
            level.put(level.wx, z, row, wx)
            level.put(level.wy, z, row, wy)
            level.put(level.wz, z, row, wz)
            level.put(level.dinv, z, row, dinv)
            level.put(level.f, z, row, f)
        return carry

    lax.fori_loop(1, planes + 1, body, 0)


def neighbours(level, src, z, row):
    u = level.get(src, z, row)
    wx = level.get(level.wx, z, row)
    total = each(lambda w, v: w * v, wx, level.right(u))
    total = each(lambda s, v: s + v, total, level.left(each(lambda w, v: w * v, wx, u)))
    mac = lambda s, w, v: s + w * v
    total = each(mac, total, level.get(level.wy, z, row), level.get(src, z, row + 1))
    total = each(mac, total, level.get(level.wy, z, row - 1), level.get(src, z, row - 1))
    total = each(mac, total, level.get(level.wz, z, row), level.get(src, z + 1, row))
    total = each(mac, total, level.get(level.wz, z - 1, row), level.get(src, z - 1, row))
    return u, total


def scaled_residual(level, src, z, row):
    u, total = neighbours(level, src, z, row)
    f = level.get(level.f, z, row)
    dinv = level.get(level.dinv, z, row)
    return u, dinv, each(lambda f_, d_, s, v: f_ + d_ * s - v, f, dinv, total, u)


def sweep(level, src, dst, planes, first, last, weights):
    keep, gain = weights

    def body(z, carry):
        for t in range(first, last):
            row = 8 * t
            u, _, r = scaled_residual(level, src, z, row)
            if keep == 0.0:
                d = each(lambda v: gain * v, r)
            else:
                d = each(lambda p, v: keep * p + gain * v, level.get(level.d, z, row), r)
            level.put(level.d, z, row, d)
            level.put(dst, z, row, each(lambda p, v: p + v, u, d))
        return carry

    lax.fori_loop(1, planes + 1, body, 0)


def start(level, planes, first, last):
    def body(z, carry):
        for t in range(first, last):
            d = each(lambda v: v * (1.0 / THETA), level.get(level.f, z, 8 * t))
            level.put(level.d, z, 8 * t, d)
            level.put(level.u, z, 8 * t, d)
        return carry

    lax.fori_loop(1, planes + 1, body, 0)


def presmooth(level, planes, first, last, degree):
    start(level, planes(0), first, last)
    src, dst = level.u, level.v
    for step, weights in enumerate(chebyshev(degree)[1:], 1):
        sweep(level, src, dst, planes(step), first, last, weights)
        src, dst = dst, src
    return src, dst


def postsmooth(level, src, dst, planes, first, last, degree):
    for step, weights in enumerate(chebyshev(degree)):
        sweep(level, src, dst, planes(step), first, last, weights)
        src, dst = dst, src
    return src, dst


def residual_pair(level, src, k, first, last, buf):
    for t in range(first, last):
        parts = []
        for z in (2 * k + 1, 2 * k + 2):
            one = Level((level.wx, level.wy, level.wz, level.f, level.dinv, level.u, level.v, level.d), level.wrap)
            _, dinv, r = scaled_residual(one, src, z, 8 * t)
            ok = dinv[0] > 0.0
            parts.append(jnp.where(ok, r[0], 0.0) / jnp.where(ok, dinv[0], 1.0))
        buf[8 * (t - first) : 8 * (t - first) + 8, :] = parts[0] + parts[1]


def pair_rows(out_rows, in_rows, out_offset, in_offset, count):
    r, c = iota(out_rows, in_rows, 0) - out_offset, iota(out_rows, in_rows, 1) - in_offset
    hit = (r >= 0) & (r < count) & ((c == 2 * r) | (c == 2 * r + 1))
    return jnp.where(hit, 1.0, 0.0).astype(F32)


def pair_lanes(in_lanes, out_lanes, in_offset, out_offset, count, weight):
    r, c = iota(in_lanes, out_lanes, 0) - in_offset, iota(in_lanes, out_lanes, 1) - out_offset
    hit = (c >= 0) & (c < count) & ((r == 2 * c) | (r == 2 * c + 1))
    return jnp.where(hit, weight, 0.0).astype(F32)


def interp(fine, coarse):
    own = jnp.right_shift(fine, 1)
    other = own + 2 * (fine - 2 * own) - 1
    return jnp.where(coarse == own, 0.75, 0.0) + jnp.where(coarse == other, 0.25, 0.0)


def pack(entries, limit=LANES):
    where, tile, offset = {}, 0, 0
    for key, n in entries:
        if n <= 0:
            continue
        if offset + n > limit:
            tile, offset = tile + 1, 0
        where[key] = (tile, offset, n)
        offset += n
    return where, tile + 1


def rows_of(entries):
    where, offset = {}, 16
    for key, n in entries:
        if n <= 0:
            continue
        where[key] = (offset, n)
        offset += n
    return where, -(-(offset + 16) // 8) * 8


def before_rows(ref, place, height):
    if place is None:
        return jnp.zeros((height, LANES), F32)
    offset, n = place
    base = offset + n - height
    value = ref[base : base + height, :]
    return jnp.where(iota(height, LANES, 0) >= height - n, value, 0.0)


def after_rows(ref, place, height):
    if place is None:
        return jnp.zeros((height, LANES), F32)
    offset, n = place
    value = ref[offset : offset + height, :]
    return jnp.where(iota(height, LANES, 0) < n, value, 0.0)


HALO = 4
HALO1 = 10
ROW0, ROW1, ROW2 = 16, 24, 8
LANE1 = 16


class Plan:
    def __init__(self, z, y, x):
        self.z, self.y, self.x = z, y, x
        z1 = z // 2
        self.z1, self.y1, self.x1 = z1, y // 2, x // 2
        reach = lambda p, n: n if p < z else max(0, n - (p - z + 1))
        self.a0 = [(("a", p), reach(p, HALO + 1)) for p in range(z + HALO + 1)]
        self.c0 = [(("c", p), reach(p, HALO)) for p in range(z + HALO)]
        self.f0 = [(("f", p), reach(p, HALO)) for p in range(z + HALO)]
        self.u0 = [(("u", p), reach(p, HALO)) for p in range(z + HALO)]
        far = lambda o, j, n: n if o == 0 else max(0, min(n, n + 2 - (z1 - j)))
        sides = [(o, j) for o in (0, 1) for j in range(z1)]
        self.sides = sides
        self.ac1 = [(("ac", o, j), far(o, j, HALO1 + 1)) for o, j in sides]
        self.a1 = [(("a1", o, j), far(o, j, HALO1 + 1)) for o, j in sides]
        self.c1 = [(("c1", o, j), far(o, j, HALO1)) for o, j in sides]
        self.f1 = [(("f1", o, j), far(o, j, HALO1)) for o, j in sides]
        self.fp = [(("fp", j), HALO1) for j in range(z1)]
        self.yrows, self.ycount = rows_of(self.a0 + self.c0 + self.f0 + self.ac1)
        self.yrows2, self.ycount2 = rows_of(self.u0 + self.fp)
        self.x0, t0 = pack(self.a0 + self.c0 + self.f0)
        self.x1m, t1 = pack(self.a1 + self.c1)
        self.xu, tu = pack(self.u0)
        self.xf, tf = pack(self.f1)
        self.e0, self.e1 = y + 16, y // 2 + 32
        self.xcount = t0 * self.e0 + t1 * self.e1
        self.xcount2 = tu * self.e0 + tf * self.e1
        self.xbase1, self.xbase2 = t0 * self.e0, tu * self.e0
        self.tiles = (t0, t1, tu, tf)
        self.r0, self.r1 = y + 32, y // 2 + 48
        self.t0, self.t1 = (1, self.r0 // 8 - 1), (1, self.r1 // 8 - 1)


def plane_of(plan, key, core, coeff, rhs, shift, zrecv):
    kind, p = key
    own = {"a": coeff, "f": rhs, "c": shift}[kind]
    if p < plan.z:
        return lambda rows: own[p + core * (plan.z - 1 - 2 * p), rows, :]
    base = {"a": 0, "c": HALO + 1, "f": 2 * HALO + 1}[kind]
    return lambda rows: zrecv[base + p - plan.z, rows, :]


def zpack(plan):
    def kernel(coeff, rhs, shift, out):
        core = lax.axis_index("pz")
        i = 0
        for ref, n in ((coeff, HALO + 1), (shift, HALO), (rhs, HALO)):
            for j in range(n):
                p = plan.z - 1 - j
                out[i] = ref[p + core * (plan.z - 1 - 2 * p)]
                i += 1

    return call(kernel, shape(3 * HALO + 1, plan.y, plan.x), ins=3)


def restrict_coefficients(plan):
    def kernel(coeff, shift, out):
        core = lax.axis_index("pz")
        ry = pair_rows(plan.y1, plan.y, 0, 0, plan.y1)
        ra = pair_lanes(LANES, LANES, 0, 0, plan.x1, 0.125)
        rc = pair_lanes(LANES, LANES, 0, plan.x1, plan.x1, 0.125)
        for k in range(plan.z1):
            i = 2 * k + core * (plan.z - 2 - 4 * k)
            a = dot(dot(ry, coeff[i] + coeff[i + 1]), ra)
            c = dot(dot(ry, shift[i] + shift[i + 1]), rc)
            out[k] = a + c

    return call(kernel, shape(plan.z1, plan.y1, LANES), ins=2)


def ypack(plan):
    def kernel(coeff, rhs, shift, zrecv, ac, aco, up, down):
        core = lax.axis_index("pz")
        for key, (offset, n) in plan.yrows.items():
            if key[0] == "ac":
                ref = (ac, aco)[key[1]]
                get, height = (lambda rows, ref=ref, j=key[2]: ref[j, rows, :]), plan.y1
            else:
                get, height = plane_of(plan, key, core, coeff, rhs, shift, zrecv), plan.y
            up[offset : offset + n, :] = get(slice(height - n, height))
            down[offset : offset + n, :] = get(slice(0, n))

    out = shape(plan.ycount, LANES)
    return call(kernel, [out, out], ins=6)


def send_lanes(out, base, extent, tile, items, rows):
    start_row = base + tile * extent
    for height, part in rows:
        lane = iota(height, LANES, 1)
        total = jnp.zeros((height, LANES), F32)
        for get, first, n, offset in items:
            value = roll(get(part), offset - first)
            total = jnp.where((lane >= offset) & (lane < offset + n), value, total)
        out[start_row : start_row + height, :] = total
        start_row += height


def xpack(plan):
    def kernel(coeff, rhs, shift, zrecv, ac, aco, before, after, up, down):
        core = lax.axis_index("pz")

        def get0(key):
            plane = plane_of(plan, key, core, coeff, rhs, shift, zrecv)
            place = plan.yrows.get(key)
            return lambda part: (
                before_rows(before, place, 8) if part == 0
                else after_rows(after, place, 8) if part == 2
                else plane(slice(0, plan.y))
            )

        def get1(key):
            place = plan.yrows.get(("ac",) + key[1:])
            ref = (ac, aco)[key[1]]
            return lambda part: (
                before_rows(before, place, 16) if part == 0
                else after_rows(after, place, 16) if part == 2
                else ref[key[2]]
            )

        for tile in range(plan.tiles[0]):
            keys = [(k, o, n) for k, (t, o, n) in plan.x0.items() if t == tile]
            rows = ((8, 0), (plan.y, 1), (8, 2))
            send_lanes(up, 0, plan.e0, tile, [(get0(k), plan.x - n, n, o) for k, o, n in keys], rows)
            send_lanes(down, 0, plan.e0, tile, [(get0(k), 0, n, o) for k, o, n in keys], rows)
        for tile in range(plan.tiles[1]):
            keys = [(k, o, n) for k, (t, o, n) in plan.x1m.items() if t == tile]
            rows = ((16, 0), (plan.y1, 1), (16, 2))
            side = lambda k: plan.x1 if k[0] == "c1" else 0
            send_lanes(up, plan.xbase1, plan.e1, tile, [(get1(k), side(k) + plan.x1 - n, n, o) for k, o, n in keys], rows)
            send_lanes(down, plan.xbase1, plan.e1, tile, [(get1(k), side(k), n, o) for k, o, n in keys], rows)

    out = shape(plan.xcount, LANES)
    return call(kernel, [out, out], ins=8)


def ypack2(plan):
    def kernel(u, zrecv, f, up, down, pair):
        for j in range(plan.z1):
            base = HALO * plan.y + j * plan.y1
            pair[j] = f[j] + zrecv[base : base + plan.y1, :]
        for key, (offset, n) in plan.yrows2.items():
            if key[0] == "fp":
                get, height = (lambda rows, j=key[1]: pair[j, rows, :]), plan.y1
            elif key[1] < plan.z:
                get, height = (lambda rows, p=key[1]: u[p, rows, :]), plan.y
            else:
                base = (key[1] - plan.z) * plan.y
                get, height = (lambda rows, b=base: zrecv[b + rows.start : b + rows.stop, :]), plan.y
            up[offset : offset + n, :] = get(slice(height - n, height))
            down[offset : offset + n, :] = get(slice(0, n))

    out = shape(plan.ycount2, LANES)
    return call(kernel, [out, out, shape(plan.z1, plan.y1, LANES)], ins=3)


def u_plane(plan, p, u, zrecv):
    if p < plan.z:
        return u[p]
    return zrecv[(p - plan.z) * plan.y : (p - plan.z + 1) * plan.y, :]


def xpack2(plan):
    def kernel(u, zrecv, pair, before, after, up, down):
        def get0(key):
            place = plan.yrows2.get(key)
            return lambda part: (
                before_rows(before, place, 8) if part == 0
                else after_rows(after, place, 8) if part == 2
                else u_plane(plan, key[1], u, zrecv)
            )

        def get1(key):
            place = plan.yrows2.get(("fp", key[2]))
            return lambda part: (
                before_rows(before, place, 16) if part == 0
                else after_rows(after, place, 16) if part == 2
                else pair[key[2]]
            )

        for tile in range(plan.tiles[2]):
            keys = [(k, o, n) for k, (t, o, n) in plan.xu.items() if t == tile]
            rows = ((8, 0), (plan.y, 1), (8, 2))
            send_lanes(up, 0, plan.e0, tile, [(get0(k), plan.x - n, n, o) for k, o, n in keys], rows)
            send_lanes(down, 0, plan.e0, tile, [(get0(k), 0, n, o) for k, o, n in keys], rows)
        for tile in range(plan.tiles[3]):
            keys = [(k, o, n) for k, (t, o, n) in plan.xf.items() if t == tile]
            rows = ((16, 0), (plan.y1, 1), (16, 2))
            send_lanes(up, plan.xbase2, plan.e1, tile, [(get1(k), k[1] * plan.x1 + plan.x1 - n, n, o) for k, o, n in keys], rows)
            send_lanes(down, plan.xbase2, plan.e1, tile, [(get1(k), k[1] * plan.x1, n, o) for k, o, n in keys], rows)

    out = shape(plan.xcount2, LANES)
    return call(kernel, [out, out], ins=5)


def zero(*refs):
    for ref in refs:
        def body(z, carry, ref=ref):
            ref[z] = jnp.zeros(ref.shape[1:], F32)
            return carry
        lax.fori_loop(0, ref.shape[0], body, 0)


def side_lanes(plan, place, before, after):
    if place is None:
        return jnp.zeros((plan.e0, LANES), F32)
    tile, offset, n = place
    rows = slice(tile * plan.e0, (tile + 1) * plan.e0)
    lane = iota(plan.e0, LANES, 1)
    value = jnp.where(lane < n, roll(after[rows, :], -offset), 0.0)
    return jnp.where(lane >= LANES - n, roll(before[rows, :], -n - offset), value)


def fill0(plan, dst, p, plane, yplace, yb, ya, xplace, xb, xa):
    top, own = ROW0 - 8, plan.y
    dst[p + 1, top:ROW0, 0:LANES] = before_rows(yb, yplace, 8)
    dst[p + 1, ROW0 : ROW0 + own, 0:LANES] = plane
    dst[p + 1, ROW0 + own : ROW0 + own + 8, 0:LANES] = after_rows(ya, yplace, 8)
    dst[p + 1, top : top + plan.e0, LANES : 2 * LANES] = side_lanes(plan, xplace, xb, xa)


def level0(plan, level, core, coeff, rhs, shift, zrecv, yb, ya, xb, xa):
    zero(level.u, level.v)
    for kind, dst, planes in (("a", level.v, plan.z + HALO + 1), ("c", level.dinv, plan.z + HALO), ("f", level.f, plan.z + HALO)):
        for p in range(planes):
            key = (kind, p)
            plane = plane_of(plan, key, core, coeff, rhs, shift, zrecv)(slice(0, plan.y))
            fill0(plan, dst, p, plane, plan.yrows.get(key), yb, ya, plan.x0.get(key), xb, xa)
    setup(level, 1.0, plan.z + HALO, *plan.t0, level.v)


def level0_scratch(plan):
    return [vmem(plan.z + HALO + 2, plan.r0, 2 * LANES)] * 8


def fill1(plan, dst, p, own, own_first, yplace, yb, ya, xplace, base, xb, xa):
    tile, offset, n = xplace
    row = ROW1 - 16
    start_row = base + tile * plan.e1
    for height, value in ((16, before_rows(yb, yplace, 16)), (plan.y1, own), (16, after_rows(ya, yplace, 16))):
        lane = iota(height, LANES, 1)
        total = jnp.where((lane >= LANE1) & (lane < LANE1 + plan.x1), roll(value, LANE1 - own_first), 0.0)
        left = roll(xb[start_row : start_row + height, :], LANE1 - n - offset)
        right = roll(xa[start_row : start_row + height, :], LANE1 + plan.x1 - offset)
        total = jnp.where((lane >= LANE1 - n) & (lane < LANE1), left, total)
        total = jnp.where((lane >= LANE1 + plan.x1) & (lane < LANE1 + plan.x1 + n), right, total)
        dst[p + 1, row : row + height, :] = total
        row, start_row = row + height, start_row + height


def down0(plan):
    def kernel(coeff, rhs, shift, zrecv, yb, ya, xb, xa, u_out, f_out, z_out, *scratch):
        buf, scratch = scratch[0], scratch[1:]
        core = lax.axis_index("pz")
        level = Level(scratch, False)
        level0(plan, level, core, coeff, rhs, shift, zrecv, yb, ya, xb, xa)
        src, _ = presmooth(level, lambda s: plan.z + HALO - s, *plan.t0, DEG)

        def keep(z, carry):
            u_out[z] = src[z + 1, ROW0 : ROW0 + plan.y, 0:LANES]
            return carry

        lax.fori_loop(0, plan.z, keep, 0)
        for j in range(HALO):
            z_out[j * plan.y : (j + 1) * plan.y, :] = src[plan.z - j, ROW0 : ROW0 + plan.y, 0:LANES]
        ry = pair_rows(plan.y1, plan.y, 0, 0, plan.y1)
        rx = pair_lanes(LANES, LANES, 0, 0, plan.x1, 0.125)
        ro = pair_lanes(LANES, LANES, 0, plan.x1, plan.x1, 0.125)

        def residual(k, carry):
            residual_pair(level, src, k, ROW0 // 8, (ROW0 + plan.y) // 8, buf)
            part = dot(ry, buf[...])
            f_out[k] = dot(part, rx)
            row = pl.multiple_of(HALO * plan.y + k * plan.y1, 8)
            z_out[pl.ds(row, plan.y1), :] = dot(part, ro)
            return carry

        lax.fori_loop(0, plan.z1, residual, 0)

    outs = [
        shape(plan.z, plan.y, LANES),
        shape(plan.z1, plan.y1, LANES),
        shape(HALO * plan.y + plan.z1 * plan.y1, LANES),
    ]
    return call(kernel, outs, [vmem(plan.y, LANES)] + level0_scratch(plan), ins=8)


def down1(plan):
    planes, z2, y2, x2 = 2 * plan.z1, plan.z1 // 2, plan.y1 // 2, plan.x1 // 2

    def kernel(ac, aco, yb, ya, xb, xa, pair, yb2, ya2, xb2, xa2, wx, wy, wz, f, dinv, u_out, message, u, d, buf):
        level = Level((wx, wy, wz, f, dinv, u, u_out, d), False)
        zero(u, u_out)
        for o, j in plan.sides:
            p = j if o == 0 else planes - 1 - j
            ref = (ac, aco)[o]
            place = plan.yrows[("ac", o, j)]
            fill1(plan, u_out, p, ref[j], 0, place, yb, ya, plan.x1m[("a1", o, j)], plan.xbase1, xb, xa)
            wide = (place[0], place[1])
            fill1c(plan, dinv, p, ref[j], wide, yb, ya, plan.x1m[("c1", o, j)], plan.xbase1, xb, xa)
            fill1(plan, f, p, pair[j], o * plan.x1, plan.yrows2[("fp", j)], yb2, ya2, plan.xf[("f1", o, j)], plan.xbase2, xb2, xa2)
        setup(level, 0.25, planes, *plan.t1, u_out)
        src, _ = presmooth(level, lambda s: planes, *plan.t1, DEG)
        assert src is u_out
        ry = pair_rows(y2, plan.y1, 0, 0, y2)
        totals = [jnp.zeros((y2, LANES), F32) for _ in range(3)]
        for k in range(z2):
            residual_pair(level, src, k, ROW1 // 8, (ROW1 + plan.y1) // 8, buf)
            own = dot(ry, ac[2 * k] + ac[2 * k + 1])
            for i, (part, first) in enumerate(((dot(ry, buf[...]), LANE1), (own, 0), (own, plan.x1))):
                totals[i] += dot(part, pair_lanes(LANES, LANES, first, k * x2, x2, 0.125))
        for i in range(3):
            message[i * y2 : (i + 1) * y2, :] = totals[i]

    big = (planes + 2, plan.r1, LANES)
    outs = [shape(*big)] * 6 + [shape(3 * y2, LANES)]
    return call(kernel, outs, [vmem(*big)] * 2 + [vmem(plan.y1, LANES)], ins=11)


def fill1c(plan, dst, p, own, yplace, yb, ya, xplace, base, xb, xa):
    fill1(plan, dst, p, own, plan.x1, yplace, yb, ya, xplace, base, xb, xa)


def prolong(level, base, out, tmp, planes, py, px):
    def body(z, carry):
        tmp[z] = dot(dot(py, base[z]), px)
        return carry

    lax.fori_loop(1, planes + 1, body, 0)


def correct(level, src, dst, tmp, fine_planes, first, last):
    for odd in (0, 1):
        def body(k, carry, odd=odd):
            z = 2 * k + 1 + odd
            for t in range(first, last):
                row = 8 * t
                near, far = level.get(tmp, k + 1, row), level.get(tmp, k + 2 * odd, row)
                dinv, u = level.get(level.dinv, z, row), level.get(src, z, row)
                new = each(lambda n, f, m, v: v + jnp.where(m > 0.0, 0.75 * n + 0.25 * f, 0.0), near, far, dinv, u)
                level.put(dst, z, row, new)
            return carry

        lax.fori_loop(0, fine_planes // 2, body, 0)


def coarse(plan, devices_y, devices_x):
    planes1 = 2 * plan.z1
    z2, y2, x2 = plan.z1 // 2, plan.y1 // 2, plan.x1 // 2
    planes2, rows2, lanes2 = 2 * z2, devices_y * y2, devices_x * x2
    planes3, rows3, lanes3 = planes2 // 2, rows2 // 2, lanes2 // 2
    h2, h3 = rows2 + 16, rows3 + 16
    t2, t3 = (1, h2 // 8 - 1), (1, h3 // 8 - 1)

    def kernel(mine, other, wx, wy, wz, f, dinv, u_in, e1, *scratch):
        l2, l3, (u1, d1, buf, tmp3, tmp2) = scratch[:8], scratch[8:16], scratch[16:]
        two, three = Level(l2, True), Level(l3, False)
        zero(two.u, two.v, *l3)
        lane = iota(y2, LANES, 1)
        for i, dst in enumerate((two.f, two.v, two.dinv)):
            for ref, plane in ((mine, lambda k: k), (other, lambda k: planes2 - 1 - k)):
                for k in range(z2):
                    for qy in range(devices_y):
                        total = jnp.zeros((y2, LANES), F32)
                        for qx in range(devices_x):
                            value = ref[qy * devices_x + qx, i * y2 : (i + 1) * y2, :]
                            value = roll(value, x2 * (qx - k))
                            total = jnp.where((lane >= x2 * qx) & (lane < x2 * qx + x2), value, total)
                        row = ROW2 + qy * y2
                        dst[plane(k) + 1, row : row + y2, :] = total
        ry = pair_rows(h3, rows2, ROW2, 0, rows3)
        rx = pair_lanes(LANES, LANES, 0, 0, lanes3, 0.125)
        for k in range(planes3):
            for src, dst in ((two.v, three.v), (two.dinv, three.dinv)):
                value = src[2 * k + 1, ROW2 : ROW2 + rows2, :] + src[2 * k + 2, ROW2 : ROW2 + rows2, :]
                dst[k + 1] = dot(dot(ry, value), rx)
        setup(two, 0.25**2, planes2, *t2, two.v)
        src2, dst2 = presmooth(two, lambda s: planes2, *t2, DEG)

        def residual(k, carry):
            residual_pair(two, src2, k, *t2, buf)
            three.f[k + 1] = dot(dot(ry, buf[...]), rx)
            return carry

        lax.fori_loop(0, planes3, residual, 0)
        setup(three, 0.25**3, planes3, *t3, three.v)
        src3, _ = presmooth(three, lambda s: planes3, *t3, CDEG)

        zero(tmp3, tmp2)
        py = interp(iota(h2, h3, 0) - ROW2, iota(h2, h3, 1) - ROW2)
        px = interp(iota(LANES, LANES, 1), iota(LANES, LANES, 0))
        prolong(two, src3, None, tmp3, planes3, py, px)
        correct(two, src2, src2, tmp3, planes2, *t2)
        src2, _ = postsmooth(two, src2, dst2, lambda s: planes2, *t2, DEG)

        me_y, me_x = lax.axis_index("py"), lax.axis_index("px")
        py = interp(iota(plan.r1, h2, 0) - ROW1 + me_y * plan.y1, iota(plan.r1, h2, 1) - ROW2)
        px = interp(iota(LANES, LANES, 1) - LANE1 + me_x * plan.x1, iota(LANES, LANES, 0))
        one = Level((wx, wy, wz, f, dinv, u1, e1, d1), False)
        zero(u1, e1)
        prolong(one, src2, None, tmp2, planes2, py, px)
        correct(one, u_in, e1, tmp2, planes1, *plan.t1)
        src1, _ = postsmooth(one, e1, u1, lambda s: min(planes1, plan.z1 + 6 - s), *plan.t1, DEG)
        assert src1 is e1

    big1 = (planes1 + 2, plan.r1, LANES)
    scratch = [vmem(planes2 + 2, h2, LANES)] * 8 + [vmem(planes3 + 2, h3, LANES)] * 8
    scratch += [vmem(*big1)] * 2 + [vmem(rows2, LANES), vmem(planes3 + 2, h2, LANES), vmem(planes2 + 2, plan.r1, LANES)]
    return call(kernel, shape(*big1), scratch, ins=8)


def up0(plan):
    planes = plan.z + HALO
    few = HALO // 2 + plan.z1 + 1

    def kernel(coeff, rhs, shift, zrecv, yb, ya, xb, xa, u_in, zrecv2, yb2, ya2, xb2, xa2, e1, out, tmp, *scratch):
        core = lax.axis_index("pz")
        level = Level(scratch, False)
        level0(plan, level, core, coeff, rhs, shift, zrecv, yb, ya, xb, xa)
        for p in range(planes):
            key = ("u", p)
            fill0(plan, level.u, p, u_plane(plan, p, u_in, zrecv2), plan.yrows2.get(key), yb2, ya2, plan.xu.get(key), xb2, xa2)
        tmp[0] = jnp.zeros(tmp.shape[1:], F32)
        fine = iota(plan.r0, plan.r1, 0) - ROW0
        py = interp(fine, iota(plan.r0, plan.r1, 1) - ROW1)
        lane = iota(LANES, 2 * LANES, 1)
        lane = jnp.where(lane < LANES + LANES // 2, lane, lane - 2 * LANES)
        px = interp(lane, iota(LANES, 2 * LANES, 0) - LANE1)
        prolong(level, e1, None, tmp, few, py, px)
        correct(level, level.u, level.u, tmp, planes, *plan.t0)
        src, _ = postsmooth(level, level.u, level.v, lambda s: planes - 1 - s, *plan.t0, DEG)
        for p in range(plan.z):
            out[p + core * (plan.z - 1 - 2 * p)] = src[p + 1, ROW0 : ROW0 + plan.y, 0:LANES]

    return call(kernel, shape(plan.z, plan.y, LANES), [vmem(few + 2, plan.r0, 2 * LANES)] + level0_scratch(plan), ins=15)


def swap(value, axis):
    return lax.ppermute(value, axis, [(0, 1), (1, 0)])


def shifted(up, down, axis):
    n = lax.axis_size(axis)
    before = lax.ppermute(up, axis, [(i, i + 1) for i in range(n - 1)])
    after = lax.ppermute(down, axis, [(i + 1, i) for i in range(n - 1)])
    return before, after


def local(rhs, coeff, shift):
    plan = Plan(*rhs.shape)
    zrecv = swap(zpack(plan)(coeff, rhs, shift), "pz")
    ac = restrict_coefficients(plan)(coeff, shift)
    aco = swap(ac, "pz")
    yb, ya = shifted(*ypack(plan)(coeff, rhs, shift, zrecv, ac, aco), "py")
    xb, xa = shifted(*xpack(plan)(coeff, rhs, shift, zrecv, ac, aco, yb, ya), "px")
    fine = (coeff, rhs, shift, zrecv, yb, ya, xb, xa)
    u, f, z_out = down0(plan)(*fine)
    zrecv2 = swap(z_out, "pz")
    up, down, pair = ypack2(plan)(u, zrecv2, f)
    yb2, ya2 = shifted(up, down, "py")
    xb2, xa2 = shifted(*xpack2(plan)(u, zrecv2, pair, yb2, ya2), "px")
    *one, message = down1(plan)(ac, aco, yb, ya, xb, xa, pair, yb2, ya2, xb2, xa2)
    ny, nx = lax.axis_size("py"), lax.axis_size("px")
    mine = lax.all_to_all(jnp.broadcast_to(message[None], (ny * nx,) + message.shape), ("py", "px"), 0, 0)
    other = swap(mine, "pz")
    e1 = coarse(plan, ny, nx)(mine, other, *one)
    return up0(plan)(*fine, u, zrecv2, yb2, ya2, xb2, xa2, e1)


lower_bound = 0.4
upper_bound = 2.0


def extended(array, sides, width):
    for axis, dim in sides:
        peers, length = (lax.axis_size(axis), array.shape[dim])
        up = [(i, (i + 1) % peers) for i in range(peers - 1)]
        down = [(j, i) for i, j in up]
        last = lax.slice_in_dim(array, length - width, length, axis=dim)
        first = lax.slice_in_dim(array, 0, width, axis=dim)
        before = lax.ppermute(last, axis, up)
        after = lax.ppermute(first, axis, down)
        array = jnp.concatenate([before, array, after], axis=dim)
    return array


def neighbour_views(shape):
    result = []
    for axis_index in range(3):
        for offset in (0, 2):
            index_list = [slice(1, 1 + shape[k]) for k in range(3)]
            index_list[axis_index] = slice(offset, offset + shape[axis_index])
            result.append(tuple(index_list))
    return result


def make_level(coeff_pad, shift_field, factor):
    center = coeff_pad[1:-1, 1:-1, 1:-1]
    weights = jnp.zeros_like(center)
    for view in neighbour_views(center.shape):
        weights = weights + 0.5 * (center + coeff_pad[view])
    inverse = 1.0 / (factor * weights + shift_field)
    return (coeff_pad, shift_field, factor, inverse)


def apply_operator(field_pad, level_data):
    coeff_pad, shift_field, factor, inverse = level_data
    center = field_pad[1:-1, 1:-1, 1:-1]
    coeff_center = coeff_pad[1:-1, 1:-1, 1:-1]
    total = jnp.zeros_like(center)
    for view in neighbour_views(center.shape):
        total = total + 0.5 * (coeff_center + coeff_pad[view]) * (center - field_pad[view])
    return factor * total + shift_field * center


def smooth(field, source, level_data, degree, padder):
    inverse = level_data[3]
    theta = 0.5 * (upper_bound + lower_bound)
    delta = 0.5 * (upper_bound - lower_bound)
    sigma = theta / delta
    rho_now = 1.0 / sigma
    if field is None:
        scaled = source * inverse
        update = scaled / theta
        field = update
    else:
        scaled = (source - apply_operator(padder(field), level_data)) * inverse
        update = scaled / theta
        field = field + update
    for sweep_index in range(degree - 1):
        scaled = (source - apply_operator(padder(field), level_data)) * inverse
        rho_next = 1.0 / (2.0 * sigma - rho_now)
        update = rho_next * rho_now * update + 2.0 * rho_next / delta * scaled
        field = field + update
        rho_now = rho_next
    return field


def restrict(field):
    s0, s1, s2 = field.shape
    return field.reshape(s0 // 2, 2, s1 // 2, 2, s2 // 2, 2).mean(axis=(1, 3, 5))


def refine_axis(padded, axis_index):
    count = padded.shape[axis_index] - 2
    center = lax.slice_in_dim(padded, 1, count + 1, axis=axis_index)
    lower = lax.slice_in_dim(padded, 0, count, axis=axis_index)
    upper = lax.slice_in_dim(padded, 2, count + 2, axis=axis_index)
    even_part = 0.75 * center + 0.25 * lower
    odd_part = 0.75 * center + 0.25 * upper
    stacked = jnp.stack([even_part, odd_part], axis=axis_index + 1)
    shape = list(center.shape)
    shape[axis_index] = 2 * count
    return stacked.reshape(shape)


def prolong_all(padded):
    for axis_index in range(3):
        padded = refine_axis(padded, axis_index)
    return padded


def fine_pad(field):
    return extended(field, (("pz", 0), ("py", 1), ("px", 2)), 1)


def face_pad(field):
    return extended(field, (("pz", 0), ("py", 1), ("px", 2)), 1)


def coarse_face_pad(field):
    return extended(field, (("pz", 0), ("py", 1), ("px", 2)), 1)


def general(rhs, coeff, shift):
    coeff_pad_zero = extended(coeff, (("pz", 0), ("py", 1), ("px", 2)), 1)
    level_zero = make_level(coeff_pad_zero, shift, 1.0)
    field = smooth(None, rhs, level_zero, DEG, fine_pad)
    residual = rhs - apply_operator(fine_pad(field), level_zero)
    fields = [field]
    sources = [rhs, restrict(residual)]
    levels_list = [None]
    coeff_now = restrict(coeff)
    shift_now = restrict(shift)
    for depth in range(1, LEVELS):
        coeff_pad = extended(coeff_now, (("pz", 0), ("py", 1), ("px", 2)), 1)
        levels_list.append(make_level(coeff_pad, shift_now, 0.25**depth))
        coeff_now = restrict(coeff_now)
        shift_now = restrict(shift_now)
    for depth in range(1, LEVELS):
        field = smooth(None, sources[depth], levels_list[depth], DEG, face_pad)
        residual = sources[depth] - apply_operator(face_pad(field), levels_list[depth])
        fields.append(field)
        sources.append(restrict(residual))
    coarse_source = sources[LEVELS]
    coarse_pad = extended(coeff_now, (("pz", 0), ("py", 1), ("px", 2)), 1)
    coarse_level = make_level(coarse_pad, shift_now, 0.25**LEVELS)
    coarse_field = smooth(None, coarse_source, coarse_level, CDEG, coarse_face_pad)
    padded = extended(coarse_field, (("pz", 0), ("py", 1), ("px", 2)), 1)
    for depth in range(LEVELS - 1, 0, -1):
        field = fields[depth] + prolong_all(padded)
        field = smooth(field, sources[depth], levels_list[depth], DEG, face_pad)
        padded = extended(field, (("pz", 0), ("py", 1), ("px", 2)), 1)
    field = fields[0] + prolong_all(padded)
    field = smooth(field, rhs, level_zero, DEG, fine_pad)
    return field


def solution(mesh):
    spec = P("pz", "py", "px")
    body = local if mesh.shape["pz"] == 2 else general

    return jax.shard_map(body, mesh=mesh, in_specs=(spec,) * 3, out_specs=spec, check_vma=False)
```

```python
import jax
import jax.numpy as jnp
from jax import lax
from jax.experimental import pallas as pl
from jax.experimental.pallas import tpu as pltpu
from jax.sharding import PartitionSpec as P

LEVELS = 3
DEG = 4
CDEG = 8
THETA = 1.2
DELTA = 0.8
F32 = jnp.float32
LANES = 128


def vmem(*shape):
    return pltpu.VMEM(shape, F32)


def shape(*dims):
    return jax.ShapeDtypeStruct(dims, F32)


def size(shape):
    total = 4
    for n in shape:
        total *= n
    return total


def call(kernel, outs, scratch=(), name=None):
    spec = pl.BlockSpec(memory_space=pltpu.VMEM)
    single = not isinstance(outs, (list, tuple))
    held = sum(size(o.shape) for o in ([outs] if single else outs)) + sum(size(r.shape) for r in scratch)

    def run(*args):
        grant = held + sum(size(a.shape) for a in args) + 4 * 1024 * 1024
        return pl.pallas_call(
            kernel,
            out_shape=outs,
            in_specs=[spec] * len(args),
            out_specs=spec if single else [spec] * len(outs),
            scratch_shapes=list(scratch),
            compiler_params=pltpu.CompilerParams(vmem_limit_bytes=min(grant, 62 * 1024 * 1024)),
            name=name,
        )(*args)

    return run


def split(value):
    high = value.astype(jnp.bfloat16)
    return high, (value - high.astype(F32)).astype(jnp.bfloat16)


def twice(matrix, axis):
    matrix = matrix.astype(jnp.bfloat16)
    return jnp.concatenate([matrix, matrix], axis=axis)


def rows_dot(matrix, value):
    return jnp.dot(matrix, jnp.concatenate(split(value), axis=0), preferred_element_type=F32)


def lanes_dot(value, matrix):
    return jnp.dot(jnp.concatenate(split(value), axis=1), matrix, preferred_element_type=F32)


def loop(count, body, unroll=1):
    if count <= unroll:
        for z in range(1, count + 1):
            body(z)
        return

    def step(i, carry):
        for j in range(unroll):
            body(i * unroll + 1 + j)
        return carry

    lax.fori_loop(0, count // unroll, step, 0)
    for z in range(count - count % unroll + 1, count + 1):
        body(z)


def iota(rows, cols, axis):
    return lax.broadcasted_iota(jnp.int32, (rows, cols), axis)


def roll(value, amount):
    amount = amount % LANES
    return value if amount == 0 else pltpu.roll(value, amount, 1)


def chebyshev(degree):
    sigma = THETA / DELTA
    rho = 1.0 / sigma
    steps = [(0.0, 1.0 / THETA)]
    for _ in range(degree - 1):
        new = 1.0 / (2.0 * sigma - rho)
        steps.append((new * rho, 2.0 * new / DELTA))
        rho = new
    return steps


class Level:
    def __init__(self, refs, tiles=1, unroll=1):
        groups = [list(refs[i : i + tiles]) for i in range(0, len(refs), tiles)]
        self.wx, self.wy, self.wz, self.f, self.dinv, self.u, self.v, self.d = groups
        self.tiles, self.unroll = tiles, unroll

    def right(self, values):
        rolled = [roll(v, -1) for v in values]
        if self.tiles == 1:
            return rolled
        lane = iota(8, LANES, 1)
        return [jnp.where(lane == LANES - 1, rolled[1 - t], rolled[t]) for t in range(2)]

    def left(self, values):
        rolled = [roll(v, 1) for v in values]
        if self.tiles == 1:
            return rolled
        lane = iota(8, LANES, 1)
        return [jnp.where(lane == 0, rolled[1 - t], rolled[t]) for t in range(2)]


def get(refs, z, row):
    return [ref[z, row : row + 8, :] for ref in refs]


def put(refs, z, row, values):
    for ref, value in zip(refs, values):
        ref[z, row : row + 8, :] = value


def each(fn, *lists):
    return [fn(*items) for items in zip(*lists)]


def setup(level, kappa, planes, rows, coef):
    half = 0.5 * kappa
    mean = lambda p, q: half * (p + q)

    for row in rows:
        put(level.wz, 0, row, each(mean, get(coef, 0, row), get(coef, 1, row)))

    def edge(z):
        row = rows[0] - 8
        put(level.wy, z, row, each(mean, get(coef, z, row), get(coef, z, row + 1)))

    loop(planes, edge, level.unroll)

    def body(z):
        for row in rows:
            a = get(coef, z, row)
            wx = each(mean, a, level.right(a))
            wy = each(mean, a, get(coef, z, row + 1))
            wz = each(mean, a, get(coef, z + 1, row))
            den = each(lambda p, q: p + q, wx, level.left(wx))
            for more in (wy, each(mean, a, get(coef, z, row - 1)), wz, each(mean, a, get(coef, z - 1, row))):
                den = each(lambda p, q: p + q, den, more)
            c = get(level.dinv, z, row)
            den = each(lambda p, q: p + q, den, c)
            dinv = each(lambda m, v: jnp.where(m > 0.0, 1.0 / jnp.where(m > 0.0, v, 1.0), 0.0), c, den)
            put(level.f, z, row, each(lambda v, w: v * w, get(level.f, z, row), dinv))
            put(level.wx, z, row, wx)
            put(level.wy, z, row, wy)
            put(level.wz, z, row, wz)
            put(level.dinv, z, row, dinv)

    loop(planes, body, level.unroll)


def scaled_residual(level, src, z, row):
    u = get(src, z, row)
    wx = get(level.wx, z, row)
    total = each(lambda w, v: w * v, wx, level.right(u))
    total = each(lambda s, v: s + v, total, level.left(each(lambda w, v: w * v, wx, u)))
    mac = lambda s, w, v: s + w * v
    total = each(mac, total, get(level.wy, z, row), get(src, z, row + 1))
    total = each(mac, total, get(level.wy, z, row - 1), get(src, z, row - 1))
    total = each(mac, total, get(level.wz, z, row), get(src, z + 1, row))
    total = each(mac, total, get(level.wz, z - 1, row), get(src, z - 1, row))
    f = get(level.f, z, row)
    dinv = get(level.dinv, z, row)
    return u, dinv, each(lambda f_, d_, s, v: f_ + d_ * s - v, f, dinv, total, u)


def sweep(level, src, dst, planes, rows, weights, last=False):
    keep, gain = weights

    def body(z):
        for row in rows:
            u, _, r = scaled_residual(level, src, z, row)
            if keep == 0.0:
                d = each(lambda v: gain * v, r)
            else:
                d = each(lambda p, v: keep * p + gain * v, get(level.d, z, row), r)
            if last:
                put(dst[:1], z, row, [u[0] + d[0]])
                continue
            put(level.d, z, row, d)
            put(dst, z, row, each(lambda p, v: p + v, u, d))

    loop(planes, body, level.unroll)


def presmooth(level, planes, rows, degree):
    def start(z):
        for row in rows:
            d = each(lambda v: v * (1.0 / THETA), get(level.f, z, row))
            put(level.d, z, row, d)
            put(level.u, z, row, d)

    loop(planes(0), start, level.unroll)
    src, dst = level.u, level.v
    for step, weights in enumerate(chebyshev(degree)[1:], 1):
        sweep(level, src, dst, planes(step), rows, weights)
        src, dst = dst, src
    return src, dst


def postsmooth(level, src, dst, planes, rows, degree, own=None):
    for step, weights in enumerate(chebyshev(degree)):
        final = step == degree - 1
        sweep(level, src, dst, planes(step), own if final and own else rows, weights, final)
        src, dst = dst, src
    return src, dst


def residual_pair(level, src, k, rows, buf):
    for i, row in enumerate(rows):
        parts = []
        for z in (2 * k + 1, 2 * k + 2):
            _, dinv, r = scaled_residual(level, src, z, row)
            ok = dinv[0] > 0.0
            parts.append(jnp.where(ok, r[0], 0.0) / jnp.where(ok, dinv[0], 1.0))
        buf[8 * i : 8 * i + 8, :] = parts[0] + parts[1]


def pair_rows(out_rows, in_rows, out_offset, in_offset, count):
    r, c = iota(out_rows, in_rows, 0) - out_offset, iota(out_rows, in_rows, 1) - in_offset
    hit = (r >= 0) & (r < count) & ((c == 2 * r) | (c == 2 * r + 1))
    return jnp.where(hit, 1.0, 0.0).astype(F32)


def pair_lanes(in_lanes, out_lanes, in_offset, out_offset, count, weight):
    r, c = iota(in_lanes, out_lanes, 0) - in_offset, iota(in_lanes, out_lanes, 1) - out_offset
    hit = (c >= 0) & (c < count) & ((r == 2 * c) | (r == 2 * c + 1))
    return jnp.where(hit, weight, 0.0).astype(F32)


def interp(fine, coarse):
    own = jnp.right_shift(fine, 1)
    other = own + 2 * (fine - 2 * own) - 1
    return jnp.where(coarse == own, 0.75, 0.0) + jnp.where(coarse == other, 0.25, 0.0)


def pack(entries, limit=LANES):
    where, tile, offset = {}, 0, 0
    for key, n in entries:
        if n <= 0:
            continue
        if offset + n > limit:
            tile, offset = tile + 1, 0
        where[key] = (tile, offset, n)
        offset += n
    return where, tile + 1


def rows_of(entries):
    where, offset = {}, 16
    for key, n in entries:
        if n <= 0:
            continue
        where[key] = (offset, n)
        offset += n
    return where, -(-(offset + 16) // 8) * 8


def before_rows(ref, place, height):
    if place is None:
        return jnp.zeros((height, LANES), F32)
    offset, n = place
    base = offset + n - height
    value = ref[base : base + height, :]
    return jnp.where(iota(height, LANES, 0) >= height - n, value, 0.0)


def after_rows(ref, place, height):
    if place is None:
        return jnp.zeros((height, LANES), F32)
    offset, n = place
    value = ref[offset : offset + height, :]
    return jnp.where(iota(height, LANES, 0) < n, value, 0.0)


HALO = 4
HALO1 = 10
ROW0, ROW1, ROW2 = 16, 24, 8


class Plan:
    def __init__(self, z, y, x):
        self.z, self.y, self.x = z, y, x
        z1 = z // 2
        self.z1, self.y1, self.x1 = z1, y // 2, x // 2
        reach = lambda p, n: n if p < z else max(0, n - (p - z + 1))
        self.a0 = [(("a", p), reach(p, HALO + 1)) for p in range(z + HALO + 1)]
        self.c0 = [(("c", p), reach(p, HALO)) for p in range(z + HALO)]
        self.f0 = [(("f", p), reach(p, HALO)) for p in range(z + HALO)]
        self.u0 = [(("u", p), reach(p, HALO)) for p in range(z + HALO)]
        far = lambda o, j, n: n if o == 0 else max(0, min(n, n + 2 - (z1 - j)))
        sides = [(o, j) for o in (0, 1) for j in range(z1)]
        self.sides = sides
        self.ac1 = [(("ac", o, j), far(o, j, HALO1 + 1)) for o, j in sides]
        self.a1 = [(("a1", o, j), far(o, j, HALO1 + 1)) for o, j in sides]
        self.c1 = [(("c1", o, j), far(o, j, HALO1)) for o, j in sides]
        self.f1 = [(("f1", o, j), far(o, j, HALO1)) for o, j in sides]
        self.fp = [(("fp", j), HALO1) for j in range(z1)]
        self.yrows, self.ycount = rows_of(self.a0 + self.c0 + self.f0 + self.ac1)
        self.yrows2, self.ycount2 = rows_of(self.u0 + self.fp)
        self.x0, t0 = pack(self.a0 + self.c0 + self.f0)
        self.x1m, t1 = pack(self.a1 + self.c1)
        self.xu, tu = pack(self.u0)
        self.xf, tf = pack(self.f1)
        self.e0, self.e1 = y + 16, y // 2 + 32
        self.xcount = t0 * self.e0 + t1 * self.e1
        self.xcount2 = tu * self.e0 + tf * self.e1
        self.xbase1, self.xbase2 = t0 * self.e0, tu * self.e0
        self.tiles = (t0, t1, tu, tf)
        self.r0, self.r1 = y + 32, y // 2 + 48
        self.own0, self.own1 = list(range(ROW0, ROW0 + y, 8)), list(range(ROW1, ROW1 + y // 2, 8))
        self.wide0 = list(range(ROW0 - HALO, ROW0 + y + HALO, 8))
        self.wide1 = list(range(ROW1 - HALO1, ROW1 + y // 2 + HALO1, 8))


def plane_of(plan, key, core, coeff, rhs, shift, zrecv):
    kind, p = key
    own = {"a": coeff, "f": rhs, "c": shift}[kind]
    if p < plan.z:
        return lambda rows: own[p + core * (plan.z - 1 - 2 * p), rows, :]
    base = {"a": 0, "c": HALO + 1, "f": 2 * HALO + 1}[kind]
    return lambda rows: zrecv[base + p - plan.z, rows, :]


def zpack(plan):
    def kernel(coeff, rhs, shift, out):
        core = lax.axis_index("pz")
        i = 0
        for ref, n in ((coeff, HALO + 1), (shift, HALO), (rhs, HALO)):
            for j in range(n):
                p = plan.z - 1 - j
                out[i] = ref[p + core * (plan.z - 1 - 2 * p)]
                i += 1

    return call(kernel, shape(3 * HALO + 1, plan.y, plan.x))


def restrict_coefficients(plan):
    def kernel(coeff, shift, out):
        core = lax.axis_index("pz")
        ry = twice(pair_rows(plan.y1, plan.y, 0, 0, plan.y1), 1)
        ra = twice(pair_lanes(LANES, LANES, 0, 0, plan.x1, 0.125), 0)
        rc = twice(pair_lanes(LANES, LANES, 0, plan.x1, plan.x1, 0.125), 0)
        for k in range(plan.z1):
            i = 2 * k + core * (plan.z - 2 - 4 * k)
            a = lanes_dot(rows_dot(ry, coeff[i] + coeff[i + 1]), ra)
            c = lanes_dot(rows_dot(ry, shift[i] + shift[i + 1]), rc)
            out[k] = a + c

    return call(kernel, shape(plan.z1, plan.y1, LANES))


def ypack(plan):
    def kernel(coeff, rhs, shift, zrecv, ac, aco, first, second, both):
        core = lax.axis_index("pz")
        up, down = stage_out(both, "py")
        for key, (offset, n) in plan.yrows.items():
            if key[0] == "ac":
                ref = (ac, aco)[key[1]]
                take, height = (lambda rows, ref=ref, j=key[2]: ref[j, rows, :]), plan.y1
            else:
                take, height = plane_of(plan, key, core, coeff, rhs, shift, zrecv), plan.y
            up[offset : offset + n, :] = take(slice(height - n, height))
            down[offset : offset + n, :] = take(slice(0, n))
        first[...], second[...] = both[0], both[1]

    out = shape(plan.ycount, LANES)
    return call(kernel, [out, out], [vmem(2, plan.ycount, LANES)])


def between(lane, first, n):
    return ((lane - first) & (LANES - 1)) < n


def send_lanes(outs, base, extent, tile, items, rows, width):
    start_row = base + tile * extent
    for height, part in rows:
        lane = iota(height, LANES, 1)
        totals = [jnp.zeros((height, LANES), F32)] * 2
        for get_part, first, n, offset in items:
            value = roll(get_part(part), offset - first)
            totals[0] = jnp.where(between(lane, offset, n), value, totals[0])
            totals[1] = jnp.where(between(lane, offset + n - width, n), value, totals[1])
        for out, total in zip(outs, totals):
            out[start_row : start_row + height, :] = total
        start_row += height


def take_lanes(before, after, rows, offset, n, last):
    lane = iota(rows.stop - rows.start, LANES, 1)
    value = jnp.where(between(lane, offset, n), before[rows, :], after[rows, :])
    return roll(value, last + 1 - n - offset)


def stage_out(both, axis):
    odd = lax.axis_index(axis) & 1
    return both.at[odd], both.at[1 - odd]


def stage_in(both, first, second, axis):
    here = lax.axis_index(axis)
    odd, size_ = here & 1, lax.axis_size(axis)
    valid = (here > 0) & (here < size_ - 1)
    both[1 - odd] = first[...]
    both[odd] = jnp.where(valid, second[...], 0.0)
    return both.at[0], both.at[1]


def xpack(plan):
    def kernel(coeff, rhs, shift, zrecv, ac, aco, ya, yb, first, second, seen, both):
        core = lax.axis_index("pz")
        before, after = stage_in(seen, ya, yb, "py")
        outs = stage_out(both, "px")

        def get0(key):
            plane = plane_of(plan, key, core, coeff, rhs, shift, zrecv)
            place = plan.yrows.get(key)
            return lambda part: (
                before_rows(before, place, 8) if part == 0
                else after_rows(after, place, 8) if part == 2
                else plane(slice(0, plan.y))
            )

        def get1(key):
            place = plan.yrows.get(("ac",) + key[1:])
            ref = (ac, aco)[key[1]]
            return lambda part: (
                before_rows(before, place, 16) if part == 0
                else after_rows(after, place, 16) if part == 2
                else ref[key[2]]
            )

        for tile in range(plan.tiles[0]):
            items = [(get0(k), plan.x - n, n, o) for k, (t, o, n) in plan.x0.items() if t == tile]
            send_lanes(outs, 0, plan.e0, tile, items, ((8, 0), (plan.y, 1), (8, 2)), plan.x)
        side = lambda k: plan.x1 if k[0] == "c1" else 0
        for tile in range(plan.tiles[1]):
            items = [(get1(k), side(k) + plan.x1 - n, n, o) for k, (t, o, n) in plan.x1m.items() if t == tile]
            send_lanes(outs, plan.xbase1, plan.e1, tile, items, ((16, 0), (plan.y1, 1), (16, 2)), plan.x1)
        first[...], second[...] = both[0], both[1]

    out = shape(plan.xcount, LANES)
    return call(kernel, [out, out], [vmem(2, plan.ycount, LANES), vmem(2, plan.xcount, LANES)])


def u_plane(plan, p, u, zrecv):
    if p < plan.z:
        return lambda rows: u[p, rows, :]
    base = (p - plan.z) * plan.y
    return lambda rows: zrecv[base + rows.start : base + rows.stop, :]


def ypack2(plan):
    def kernel(u, zrecv, f, first, second, pair, both):
        up, down = stage_out(both, "py")
        for j in range(plan.z1):
            base = HALO * plan.y + j * plan.y1
            pair[j] = f[j] + zrecv[base : base + plan.y1, :]
        for key, (offset, n) in plan.yrows2.items():
            if key[0] == "fp":
                take, height = (lambda rows, j=key[1]: pair[j, rows, :]), plan.y1
            else:
                take, height = u_plane(plan, key[1], u, zrecv), plan.y
            up[offset : offset + n, :] = take(slice(height - n, height))
            down[offset : offset + n, :] = take(slice(0, n))
        first[...], second[...] = both[0], both[1]

    out = shape(plan.ycount2, LANES)
    return call(kernel, [out, out, shape(plan.z1, plan.y1, LANES)], [vmem(2, plan.ycount2, LANES)])


def xpack2(plan):
    def kernel(u, zrecv, pair, ya, yb, first, second, seen, both):
        before, after = stage_in(seen, ya, yb, "py")
        outs = stage_out(both, "px")

        def get0(key):
            place = plan.yrows2.get(key)
            plane = u_plane(plan, key[1], u, zrecv)
            return lambda part: (
                before_rows(before, place, 8) if part == 0
                else after_rows(after, place, 8) if part == 2
                else plane(slice(0, plan.y))
            )

        def get1(key):
            place = plan.yrows2.get(("fp", key[2]))
            return lambda part: (
                before_rows(before, place, 16) if part == 0
                else after_rows(after, place, 16) if part == 2
                else pair[key[2]]
            )

        for tile in range(plan.tiles[2]):
            items = [(get0(k), plan.x - n, n, o) for k, (t, o, n) in plan.xu.items() if t == tile]
            send_lanes(outs, 0, plan.e0, tile, items, ((8, 0), (plan.y, 1), (8, 2)), plan.x)
        for tile in range(plan.tiles[3]):
            items = [(get1(k), k[1] * plan.x1 + plan.x1 - n, n, o) for k, (t, o, n) in plan.xf.items() if t == tile]
            send_lanes(outs, plan.xbase2, plan.e1, tile, items, ((16, 0), (plan.y1, 1), (16, 2)), plan.x1)
        first[...], second[...] = both[0], both[1]

    out = shape(plan.xcount2, LANES)
    return call(kernel, [out, out], [vmem(2, plan.ycount2, LANES), vmem(2, plan.xcount2, LANES)])


def zero(*groups):
    for ref in [ref for group in groups for ref in group]:
        def body(z, ref=ref):
            ref[z - 1] = jnp.zeros(ref.shape[1:], F32)
        loop(ref.shape[0], body)


def fill0(plan, dst, p, plane, yplace, before, after, xplace, left, right):
    main, side = dst
    top, own = ROW0 - 8, plan.y
    main[p + 1, top:ROW0, :] = before_rows(before, yplace, 8)
    main[p + 1, ROW0 : ROW0 + own, :] = plane(slice(0, own))
    main[p + 1, ROW0 + own : ROW0 + own + 8, :] = after_rows(after, yplace, 8)
    value = jnp.zeros((plan.e0, LANES), F32)
    if xplace is not None:
        tile, offset, n = xplace
        rows = slice(tile * plan.e0, (tile + 1) * plan.e0)
        value = take_lanes(left, right, rows, offset, n, LANES - 1)
        value = jnp.where(between(iota(plan.e0, LANES, 1), -n, 2 * n), value, 0.0)
    side[p + 1, top : top + plan.e0, :] = value


def level0(plan, level, core, coeff, rhs, shift, zrecv, before, after, left, right):
    zero(level.u, level.v)
    for kind, dst, planes in (("a", level.v, plan.z + HALO + 1), ("c", level.dinv, plan.z + HALO), ("f", level.f, plan.z + HALO)):
        for p in range(planes):
            key = (kind, p)
            plane = plane_of(plan, key, core, coeff, rhs, shift, zrecv)
            fill0(plan, dst, p, plane, plan.yrows.get(key), before, after, plan.x0.get(key), left, right)
    setup(level, 1.0, plan.z + HALO, plan.wide0, level.v)


def level0_scratch(plan):
    return [vmem(plan.z + HALO + 2, plan.r0, LANES)] * 16


def fill1(plan, dst, p, own, own_first, yplace, before, after, xplace, base, left, right):
    tile, offset, n = xplace
    row = ROW1 - 16
    start_row = base + tile * plan.e1
    for height, value in ((16, before_rows(before, yplace, 16)), (plan.y1, own), (16, after_rows(after, yplace, 16))):
        lane = iota(height, LANES, 1)
        halo = take_lanes(left, right, slice(start_row, start_row + height), offset, n, LANES - 1)
        halo = jnp.where(between(lane, -n, n) | between(lane, plan.x1, n), halo, 0.0)
        dst[p + 1, row : row + height, :] = jnp.where(lane < plan.x1, roll(value, -own_first), halo)
        row, start_row = row + height, start_row + height


def down0(plan):
    def kernel(coeff, rhs, shift, zrecv, ya, yb, xa, xb, u_out, f_out, z_out, seen_y, seen_x, buf, *scratch):
        core = lax.axis_index("pz")
        ends = stage_in(seen_y, ya, yb, "py") + stage_in(seen_x, xa, xb, "px")
        level = Level(scratch, 2)
        level0(plan, level, core, coeff, rhs, shift, zrecv, *ends)
        src, _ = presmooth(level, lambda s: plan.z + HALO - s, plan.wide0, DEG)
        main = src[0]

        def keep(z):
            u_out[z - 1] = main[z, ROW0 : ROW0 + plan.y, :]

        loop(plan.z, keep)
        for j in range(HALO):
            z_out[j * plan.y : (j + 1) * plan.y, :] = main[plan.z - j, ROW0 : ROW0 + plan.y, :]
        ry = twice(pair_rows(plan.y1, plan.y, 0, 0, plan.y1), 1)
        rx = twice(pair_lanes(LANES, LANES, 0, 0, plan.x1, 0.125), 0)
        ro = twice(pair_lanes(LANES, LANES, 0, plan.x1, plan.x1, 0.125), 0)

        def residual(z):
            residual_pair(level, src, z - 1, plan.own0, buf)
            part = rows_dot(ry, buf[...])
            f_out[z - 1] = lanes_dot(part, rx)
            row = HALO * plan.y + (z - 1) * plan.y1
            z_out[pl.ds(pl.multiple_of(row, 8), plan.y1), :] = lanes_dot(part, ro)

        loop(plan.z1, residual)

    outs = [
        shape(plan.z, plan.y, LANES),
        shape(plan.z1, plan.y1, LANES),
        shape(HALO * plan.y + plan.z1 * plan.y1, LANES),
    ]
    seen = [vmem(2, plan.ycount, LANES), vmem(2, plan.xcount, LANES)]
    return call(kernel, outs, seen + [vmem(plan.y, LANES)] + level0_scratch(plan))


def down1(plan):
    planes, z2, y2, x2 = 2 * plan.z1, plan.z1 // 2, plan.y1 // 2, plan.x1 // 2

    def kernel(ac, aco, ya, yb, xa, xb, pair, ya2, yb2, xa2, xb2, wx, wy, wz, f, dinv, u_out, message, *scratch):
        seen_y, seen_x, seen_y2, seen_x2, u, d, buf = scratch
        yends, xends = stage_in(seen_y, ya, yb, "py"), stage_in(seen_x, xa, xb, "px")
        yends2, xends2 = stage_in(seen_y2, ya2, yb2, "py"), stage_in(seen_x2, xa2, xb2, "px")
        level = Level((wx, wy, wz, f, dinv, u, u_out, d), 1, 2)
        zero(level.u, level.v)
        for o, j in plan.sides:
            p = j if o == 0 else planes - 1 - j
            own, place = (ac, aco)[o][j], plan.yrows[("ac", o, j)]
            fill1(plan, u_out, p, own, 0, place, *yends, plan.x1m[("a1", o, j)], plan.xbase1, *xends)
            fill1(plan, dinv, p, own, plan.x1, place, *yends, plan.x1m[("c1", o, j)], plan.xbase1, *xends)
            fill1(plan, f, p, pair[j], o * plan.x1, plan.yrows2[("fp", j)], *yends2, plan.xf[("f1", o, j)], plan.xbase2, *xends2)
        setup(level, 0.25, planes, plan.wide1, level.v)
        src, _ = presmooth(level, lambda s: planes, plan.wide1, DEG)
        assert src[0] is u_out
        ry = twice(pair_rows(y2, plan.y1, 0, 0, y2), 1)
        totals = [jnp.zeros((y2, LANES), F32) for _ in range(3)]
        for k in range(z2):
            residual_pair(level, src, k, plan.own1, buf)
            own = rows_dot(ry, ac[2 * k] + ac[2 * k + 1])
            for i, (part, first) in enumerate(((rows_dot(ry, buf[...]), 0), (own, 0), (own, plan.x1))):
                totals[i] += lanes_dot(part, twice(pair_lanes(LANES, LANES, first, k * x2, x2, 0.125), 0))
        for i in range(3):
            message[i * y2 : (i + 1) * y2, :] = totals[i]

    big = (planes + 2, plan.r1, LANES)
    outs = [shape(*big)] * 6 + [shape(3 * y2, LANES)]
    seen = [vmem(2, n, LANES) for n in (plan.ycount, plan.xcount, plan.ycount2, plan.xcount2)]
    return call(kernel, outs, seen + [vmem(*big)] * 2 + [vmem(plan.y1, LANES)])


def prolong(src, tmp, planes, py, px, rows, unroll=1):
    def body(z):
        for out, matrix in zip(tmp, px):
            out[z, rows, :] = rows_dot(py, lanes_dot(src[z], matrix))

    loop(planes, body, unroll)


def correct(level, src, dst, tmp, fine_planes, rows):
    def body(k):
        for row in rows:
            own = each(lambda v: 0.75 * v, get(tmp, k, row))
            for z, far in ((2 * k - 1, k - 1), (2 * k, k + 1)):
                new = each(
                    lambda n, f, m, v: v + jnp.where(m > 0.0, n + 0.25 * f, 0.0),
                    own, get(tmp, far, row), get(level.dinv, z, row), get(src, z, row),
                )
                put(dst, z, row, new)

    loop(fine_planes // 2, body, level.unroll)


def coarse(plan):
    planes1 = 2 * plan.z1
    z2, y2, x2 = plan.z1 // 2, plan.y1 // 2, plan.x1 // 2
    planes2, rows2, lanes2 = 2 * z2, 3 * y2, 3 * x2
    planes3, rows3, lanes3 = planes2 // 2, rows2 // 2, lanes2 // 2
    h2, h3 = rows2 + 16, rows3 + 16
    wide2, wide3 = list(range(ROW2, ROW2 + rows2, 8)), list(range(ROW2, ROW2 + rows3, 8))
    block = 3 * y2

    def kernel(own, xa, xb, owno, xao, xbo, wx, wy, wz, f, dinv, u_in, e1, *scratch):
        l2, l3, (u1, d1, buf, tmp3, tmp2, seen) = scratch[:8], scratch[8:16], scratch[16:]
        two, three = Level(l2, 1, 4), Level(l3, 1, 8)
        zero(two.u, two.v, [*l3])
        odd = lax.axis_index("py") & 1
        here = lax.axis_index("py")
        parts = ((1 - odd) * 2, 1, odd * 2)
        edge = (here > 0) & (here < lax.axis_size("py") - 1)
        ok = (jnp.where(odd == 1, True, edge), None, jnp.where(odd == 0, True, edge))
        lane = iota(y2, LANES, 1)
        group = [between(lane, x2 * g, x2) for g in range(4)]
        for side, (mid, first, second) in enumerate(((own, xa, xb), (owno, xao, xbo))):
            left, right = stage_in(seen, first, second, "px")
            for i, dst in enumerate((two.f[0], two.v[0], two.dinv[0])):
                for b in range(3):
                    base = pl.multiple_of(parts[b] * block + i * y2, 8)
                    blocks = [ref[pl.ds(base, y2), :] for ref in (left, mid, right)]
                    if ok[b] is not None:
                        blocks = [jnp.where(ok[b], v, 0.0) for v in blocks]
                    turned = []
                    for s in range(4):
                        value = jnp.zeros((y2, LANES), F32)
                        for k in range(z2):
                            if (k + s) % 4 < 3:
                                value = jnp.where(group[k], blocks[(k + s) % 4], value)
                        turned.append(roll(value, x2 * s))
                    for k in range(z2):
                        value = jnp.zeros((y2, LANES), F32)
                        for g in range(3):
                            value = jnp.where(group[g], turned[(g - k) % 4], value)
                        p = k if side == 0 else planes2 - 1 - k
                        dst[p + 1, ROW2 + b * y2 : ROW2 + (b + 1) * y2, :] = value
        ry = twice(pair_rows(h3, rows2, ROW2, 0, rows3), 1)
        rx = twice(pair_lanes(LANES, LANES, 0, 0, lanes3, 0.125), 0)
        for k in range(planes3):
            for src, dst in ((two.v[0], three.v[0]), (two.dinv[0], three.dinv[0])):
                value = src[2 * k + 1, ROW2 : ROW2 + rows2, :] + src[2 * k + 2, ROW2 : ROW2 + rows2, :]
                dst[k + 1] = lanes_dot(rows_dot(ry, value), rx)
        setup(two, 0.25**2, planes2, wide2, two.v)
        src2, dst2 = presmooth(two, lambda s: planes2, wide2, DEG)
        for k in range(planes3):
            residual_pair(two, src2, k, wide2, buf.at[k])
        for k in range(planes3):
            three.f[0][k + 1] = lanes_dot(rows_dot(ry, buf[k]), rx)
        setup(three, 0.25**3, planes3, wide3, three.v)
        src3, _ = presmooth(three, lambda s: planes3, wide3, CDEG)

        zero([tmp3, tmp2])
        px = twice(interp(iota(LANES, LANES, 1), iota(LANES, LANES, 0)), 0)
        py = twice(interp(iota(h2, h3, 0) - ROW2, iota(h2, h3, 1) - ROW2), 1)
        prolong(src3[0], [tmp3], planes3, py, [px], slice(0, h2), 4)
        correct(two, src2, src2, [tmp3], planes2, wide2)
        src2, _ = postsmooth(two, src2, dst2, lambda s: planes2, wide2, DEG)

        lanes = iota(LANES, LANES, 1)
        lanes = jnp.where(lanes < LANES - 2 * x2 + 16, lanes, lanes - LANES) + 2 * x2
        px = twice(interp(lanes, iota(LANES, LANES, 0)), 0)
        py = twice(interp(iota(plan.r1, h2, 0) - ROW1 + 2 * y2, iota(plan.r1, h2, 1) - ROW2), 1)
        one = Level((wx, wy, wz, f, dinv, u1, e1, d1), 1, 2)
        zero(one.u, one.v)
        prolong(src2[0], [tmp2], planes2, py, [px], slice(0, plan.r1), 2)
        correct(one, [u_in], one.v, [tmp2], planes1, plan.wide1)
        src1, _ = postsmooth(one, one.v, one.u, lambda s: min(planes1, plan.z1 + 6 - s), plan.wide1, DEG)
        assert src1[0] is e1

    big1 = (planes1 + 2, plan.r1, LANES)
    scratch = [vmem(planes2 + 2, h2, LANES)] * 8 + [vmem(planes3 + 2, h3, LANES)] * 8 + [vmem(*big1)] * 2
    scratch += [vmem(planes3, rows2, LANES), vmem(planes3 + 2, h2, LANES), vmem(planes2 + 2, plan.r1, LANES)]
    scratch += [vmem(2, 3 * block, LANES)]
    return call(kernel, shape(*big1), scratch)


def up0(plan):
    planes = plan.z + HALO
    few = HALO // 2 + plan.z1 + 1

    def kernel(coeff, rhs, shift, zrecv, ya, yb, xa, xb, u_in, zrecv2, ya2, yb2, xa2, xb2, e1, out, *scratch):
        seen_y, seen_x, seen_y2, seen_x2, tmp, tmps = scratch[:6]
        core = lax.axis_index("pz")
        ends = stage_in(seen_y, ya, yb, "py") + stage_in(seen_x, xa, xb, "px")
        ends2 = stage_in(seen_y2, ya2, yb2, "py") + stage_in(seen_x2, xa2, xb2, "px")
        level = Level(scratch[6:], 2)
        level0(plan, level, core, coeff, rhs, shift, zrecv, *ends)
        for p in range(planes):
            key = ("u", p)
            plane = u_plane(plan, p, u_in, zrecv2)
            fill0(plan, level.u, p, plane, plan.yrows2.get(key), *ends2[:2], plan.xu.get(key), *ends2[2:])
        tmp[0] = jnp.zeros(tmp.shape[1:], F32)
        tmps[0] = jnp.zeros(tmp.shape[1:], F32)
        first, count = plan.wide0[0], 8 * len(plan.wide0)
        py = twice(interp(iota(count, plan.r1, 0) + first - ROW0, iota(count, plan.r1, 1) - ROW1), 1)
        lane = iota(LANES, LANES, 1)
        coarse_lane = iota(LANES, LANES, 0)
        coarse_lane = jnp.where(coarse_lane < plan.x1 + 16, coarse_lane, coarse_lane - LANES)
        main = twice(interp(lane, coarse_lane), 0)
        side = twice(interp(jnp.where(lane < LANES // 2, lane + LANES, lane - LANES), coarse_lane), 0)
        prolong(e1, [tmp, tmps], few, py, [main, side], slice(first, first + count))
        correct(level, level.u, level.u, [tmp, tmps], planes, plan.wide0)
        src, _ = postsmooth(level, level.u, level.v, lambda s: planes - 1 - s, plan.wide0, DEG, plan.own0)
        for p in range(plan.z):
            out[p + core * (plan.z - 1 - 2 * p)] = src[0][p + 1, ROW0 : ROW0 + plan.y, :]

    seen = [vmem(2, n, LANES) for n in (plan.ycount, plan.xcount, plan.ycount2, plan.xcount2)]
    tmps = [vmem(few + 2, plan.r0, LANES)] * 2
    return call(kernel, shape(plan.z, plan.y, LANES), seen + tmps + level0_scratch(plan))


def swap(value, axis):
    return lax.ppermute(value, axis, [(0, 1), (1, 0)])


def meet(first, second, axis):
    n = lax.axis_size(axis)
    even = [(i, i + 1) for i in range(0, n, 2)]
    odd = [(i, (i + 1) % n) for i in range(1, n, 2)]
    both = lambda pairs: pairs + [(j, i) for i, j in pairs]
    return lax.ppermute(first, axis, both(even)), lax.ppermute(second, axis, both(odd))


def local(rhs, coeff, shift):
    plan = Plan(*rhs.shape)
    zrecv = swap(zpack(plan)(coeff, rhs, shift), "pz")
    ac = restrict_coefficients(plan)(coeff, shift)
    aco = swap(ac, "pz")
    ends_y = meet(*ypack(plan)(coeff, rhs, shift, zrecv, ac, aco), "py")
    ends_x = meet(*xpack(plan)(coeff, rhs, shift, zrecv, ac, aco, *ends_y), "px")
    fine = (coeff, rhs, shift, zrecv, *ends_y, *ends_x)
    u, f, z_out = down0(plan)(*fine)
    zrecv2 = swap(z_out, "pz")
    first, second, pair = ypack2(plan)(u, zrecv2, f)
    ends_y2 = meet(first, second, "py")
    ends_x2 = meet(*xpack2(plan)(u, zrecv2, pair, *ends_y2), "px")
    *one, message = down1(plan)(ac, aco, *ends_y, *ends_x, pair, *ends_y2, *ends_x2)
    first, second = meet(message, message, "py")
    wide = jnp.concatenate([first, message, second])
    blocks = (wide, *meet(wide, wide, "px"))
    e1 = coarse(plan)(*blocks, *[swap(b, "pz") for b in blocks], *one)
    return up0(plan)(*fine, u, zrecv2, *ends_y2, *ends_x2, e1)


lower_bound = 0.4
upper_bound = 2.0


def extended(array, sides, width):
    for axis, dim in sides:
        peers, length = (lax.axis_size(axis), array.shape[dim])
        up = [(i, (i + 1) % peers) for i in range(peers - 1)]
        down = [(j, i) for i, j in up]
        last = lax.slice_in_dim(array, length - width, length, axis=dim)
        first = lax.slice_in_dim(array, 0, width, axis=dim)
        before = lax.ppermute(last, axis, up)
        after = lax.ppermute(first, axis, down)
        array = jnp.concatenate([before, array, after], axis=dim)
    return array


def neighbour_views(shape):
    result = []
    for axis_index in range(3):
        for offset in (0, 2):
            index_list = [slice(1, 1 + shape[k]) for k in range(3)]
            index_list[axis_index] = slice(offset, offset + shape[axis_index])
            result.append(tuple(index_list))
    return result


def make_level(coeff_pad, shift_field, factor):
    center = coeff_pad[1:-1, 1:-1, 1:-1]
    weights = jnp.zeros_like(center)
    for view in neighbour_views(center.shape):
        weights = weights + 0.5 * (center + coeff_pad[view])
    inverse = 1.0 / (factor * weights + shift_field)
    return (coeff_pad, shift_field, factor, inverse)


def apply_operator(field_pad, level_data):
    coeff_pad, shift_field, factor, inverse = level_data
    center = field_pad[1:-1, 1:-1, 1:-1]
    coeff_center = coeff_pad[1:-1, 1:-1, 1:-1]
    total = jnp.zeros_like(center)
    for view in neighbour_views(center.shape):
        total = total + 0.5 * (coeff_center + coeff_pad[view]) * (center - field_pad[view])
    return factor * total + shift_field * center


def smooth(field, source, level_data, degree, padder):
    inverse = level_data[3]
    theta = 0.5 * (upper_bound + lower_bound)
    delta = 0.5 * (upper_bound - lower_bound)
    sigma = theta / delta
    rho_now = 1.0 / sigma
    if field is None:
        scaled = source * inverse
        update = scaled / theta
        field = update
    else:
        scaled = (source - apply_operator(padder(field), level_data)) * inverse
        update = scaled / theta
        field = field + update
    for sweep_index in range(degree - 1):
        scaled = (source - apply_operator(padder(field), level_data)) * inverse
        rho_next = 1.0 / (2.0 * sigma - rho_now)
        update = rho_next * rho_now * update + 2.0 * rho_next / delta * scaled
        field = field + update
        rho_now = rho_next
    return field


def restrict(field):
    s0, s1, s2 = field.shape
    return field.reshape(s0 // 2, 2, s1 // 2, 2, s2 // 2, 2).mean(axis=(1, 3, 5))


def refine_axis(padded, axis_index):
    count = padded.shape[axis_index] - 2
    center = lax.slice_in_dim(padded, 1, count + 1, axis=axis_index)
    lower = lax.slice_in_dim(padded, 0, count, axis=axis_index)
    upper = lax.slice_in_dim(padded, 2, count + 2, axis=axis_index)
    even_part = 0.75 * center + 0.25 * lower
    odd_part = 0.75 * center + 0.25 * upper
    stacked = jnp.stack([even_part, odd_part], axis=axis_index + 1)
    shape = list(center.shape)
    shape[axis_index] = 2 * count
    return stacked.reshape(shape)


def prolong_all(padded):
    for axis_index in range(3):
        padded = refine_axis(padded, axis_index)
    return padded


def fine_pad(field):
    return extended(field, (("pz", 0), ("py", 1), ("px", 2)), 1)


def face_pad(field):
    return extended(field, (("pz", 0), ("py", 1), ("px", 2)), 1)


def coarse_face_pad(field):
    return extended(field, (("pz", 0), ("py", 1), ("px", 2)), 1)


def general(rhs, coeff, shift):
    coeff_pad_zero = extended(coeff, (("pz", 0), ("py", 1), ("px", 2)), 1)
    level_zero = make_level(coeff_pad_zero, shift, 1.0)
    field = smooth(None, rhs, level_zero, DEG, fine_pad)
    residual = rhs - apply_operator(fine_pad(field), level_zero)
    fields = [field]
    sources = [rhs, restrict(residual)]
    levels_list = [None]
    coeff_now = restrict(coeff)
    shift_now = restrict(shift)
    for depth in range(1, LEVELS):
        coeff_pad = extended(coeff_now, (("pz", 0), ("py", 1), ("px", 2)), 1)
        levels_list.append(make_level(coeff_pad, shift_now, 0.25**depth))
        coeff_now = restrict(coeff_now)
        shift_now = restrict(shift_now)
    for depth in range(1, LEVELS):
        field = smooth(None, sources[depth], levels_list[depth], DEG, face_pad)
        residual = sources[depth] - apply_operator(face_pad(field), levels_list[depth])
        fields.append(field)
        sources.append(restrict(residual))
    coarse_source = sources[LEVELS]
    coarse_pad = extended(coeff_now, (("pz", 0), ("py", 1), ("px", 2)), 1)
    coarse_level = make_level(coarse_pad, shift_now, 0.25**LEVELS)
    coarse_field = smooth(None, coarse_source, coarse_level, CDEG, coarse_face_pad)
    padded = extended(coarse_field, (("pz", 0), ("py", 1), ("px", 2)), 1)
    for depth in range(LEVELS - 1, 0, -1):
        field = fields[depth] + prolong_all(padded)
        field = smooth(field, sources[depth], levels_list[depth], DEG, face_pad)
        padded = extended(field, (("pz", 0), ("py", 1), ("px", 2)), 1)
    field = fields[0] + prolong_all(padded)
    field = smooth(field, rhs, level_zero, DEG, fine_pad)
    return field


def solution(mesh):
    spec = P("pz", "py", "px")
    body = local if mesh.shape["pz"] == 2 else general

    return jax.shard_map(body, mesh=mesh, in_specs=(spec,) * 3, out_specs=spec, check_vma=False)
```

```python
import jax
import jax.numpy as jnp
from jax import lax
from jax.experimental import pallas as pl
from jax.experimental.pallas import tpu as pltpu
from jax.sharding import PartitionSpec as P

LEVELS = 3
DEG = 4
CDEG = 8
THETA = 1.2
DELTA = 0.8
F32 = jnp.float32
LANES = 128


def vmem(*shape):
    return pltpu.VMEM(shape, F32)


def even(n):
    return n + n % 2


def shape(*dims):
    return jax.ShapeDtypeStruct(dims, F32)


def size(shape):
    total = 4
    for n in shape:
        total *= n
    return total


def call(kernel, outs, scratch=(), raw=False, tight=True):
    spec = pl.BlockSpec(memory_space=pltpu.VMEM)
    source = pl.BlockSpec(memory_space=pl.ANY) if raw else spec
    single = not isinstance(outs, (list, tuple))
    outer = sum(size(o.shape) for o in ([outs] if single else outs))
    held = sum(size(r.shape) for r in scratch if not raw)

    def run(*args):
        grant = (held if tight else held + outer + sum(size(a.shape) for a in args if not raw)) + 3 * 1024 * 1024
        return pl.pallas_call(
            kernel,
            out_shape=outs,
            in_specs=[source] * len(args),
            out_specs=spec if single else [spec] * len(outs),
            scratch_shapes=list(scratch),
            compiler_params=pltpu.CompilerParams(vmem_limit_bytes=min(grant, 62 * 1024 * 1024)),
        )(*args)

    return run


def split(value):
    high = value.astype(jnp.bfloat16)
    return high, (value - high.astype(F32)).astype(jnp.bfloat16)


def twice(matrix, axis):
    matrix = matrix.astype(jnp.bfloat16)
    return jnp.concatenate([matrix, matrix], axis=axis)


def rows_dot(matrix, value):
    return jnp.dot(matrix, jnp.concatenate(split(value), axis=0), preferred_element_type=F32)


def lanes_dot(value, matrix):
    return jnp.dot(jnp.concatenate(split(value), axis=1), matrix, preferred_element_type=F32)


def loop(count, body, group=1):
    if count <= group:
        body(1, count)
        return

    def step(i, carry):
        body(i * group + 1, group)
        return carry

    lax.fori_loop(0, count // group, step, 0)
    if count % group:
        body(count - count % group + 1, count % group)


def iota(rows, cols, axis):
    return lax.broadcasted_iota(jnp.int32, (rows, cols), axis)


def roll(value, amount):
    amount = amount % LANES
    return value if amount == 0 else pltpu.roll(value, amount, 1)


def chebyshev(degree):
    sigma = THETA / DELTA
    rho = 1.0 / sigma
    steps = [(0.0, 1.0 / THETA)]
    for _ in range(degree - 1):
        new = 1.0 / (2.0 * sigma - rho)
        steps.append((new * rho, 2.0 * new / DELTA))
        rho = new
    return steps


class Level:
    def __init__(self, refs, tiles=1, group=2):
        groups = [list(refs[i : i + tiles]) for i in range(0, len(refs), tiles)]
        self.wx, self.wy, self.wz, self.f, self.dinv, self.u, self.v, self.d = groups
        self.tiles, self.group = tiles, group

    def right(self, values):
        rolled = [roll(v, -1) for v in values]
        if self.tiles == 1:
            return rolled
        lane = iota(8, LANES, 1)
        return [jnp.where(lane == LANES - 1, rolled[1 - t], rolled[t]) for t in range(2)]

    def left(self, values):
        rolled = [roll(v, 1) for v in values]
        if self.tiles == 1:
            return rolled
        lane = iota(8, LANES, 1)
        return [jnp.where(lane == 0, rolled[1 - t], rolled[t]) for t in range(2)]


def get(refs, z, row):
    return [ref[z, row : row + 8, :] for ref in refs]


def put(refs, z, row, values):
    for ref, value in zip(refs, values):
        ref[z, row : row + 8, :] = value


def each(fn, *lists):
    return [fn(*items) for items in zip(*lists)]


def setup(level, kappa, planes, rows, coef):
    half = 0.5 * kappa
    mean = lambda p, q: half * (p + q)

    for row in rows:
        put(level.wz, 0, row, each(mean, get(coef, 0, row), get(coef, 1, row)))

    def edge(z, n):
        row = rows[0] - 8
        for i in range(n):
            put(level.wy, z + i, row, each(mean, get(coef, z + i, row), get(coef, z + i, row + 1)))

    loop(planes, edge, level.group)

    def body(z, n):
        for row in rows:
            column = [get(coef, z + i, row) for i in range(-1, n + 1)]
            faces = [each(mean, p, q) for p, q in zip(column, column[1:])]
            for i in range(n):
                a = column[i + 1]
                wx = each(mean, a, level.right(a))
                wy = each(mean, a, get(coef, z + i, row + 1))
                den = each(lambda p, q: p + q, wx, level.left(wx))
                for more in (wy, each(mean, a, get(coef, z + i, row - 1)), faces[i], faces[i + 1]):
                    den = each(lambda p, q: p + q, den, more)
                c = get(level.dinv, z + i, row)
                den = each(lambda p, q: p + q, den, c)
                dinv = each(lambda m, v: jnp.where(m > 0.0, 1.0 / jnp.where(m > 0.0, v, 1.0), 0.0), c, den)
                put(level.f, z + i, row, each(lambda v, w: v * w, get(level.f, z + i, row), dinv))
                put(level.wx, z + i, row, wx)
                put(level.wy, z + i, row, wy)
                put(level.wz, z + i, row, faces[i + 1])
                put(level.dinv, z + i, row, dinv)

    loop(planes, body, level.group)


def scaled_residual(level, src, z, n, row):
    column = [get(src, z + i, row) for i in range(-1, n + 1)]
    faces = [get(level.wz, z + i, row) for i in range(-1, n)]
    mac = lambda s, w, v: s + w * v
    result = []
    for i in range(n):
        u = column[i + 1]
        wx = get(level.wx, z + i, row)
        total = each(lambda w, v: w * v, wx, level.right(u))
        total = each(lambda s, v: s + v, total, level.left(each(lambda w, v: w * v, wx, u)))
        total = each(mac, total, get(level.wy, z + i, row), get(src, z + i, row + 1))
        total = each(mac, total, get(level.wy, z + i, row - 1), get(src, z + i, row - 1))
        total = each(mac, total, faces[i + 1], column[i + 2])
        total = each(mac, total, faces[i], column[i])
        f = get(level.f, z + i, row)
        dinv = get(level.dinv, z + i, row)
        result.append((u, dinv, each(lambda f_, d_, s, v: f_ + d_ * s - v, f, dinv, total, u)))
    return result


def sweep(level, src, dst, planes, rows, weights, last=False):
    keep, gain = weights

    def body(z, n):
        for row in rows:
            for i, (u, _, r) in enumerate(scaled_residual(level, src, z, n, row)):
                if keep == 0.0:
                    d = each(lambda v: gain * v, r)
                else:
                    d = each(lambda p, v: keep * p + gain * v, get(level.d, z + i, row), r)
                if last:
                    put(dst[:1], z + i, row, [u[0] + d[0]])
                    continue
                put(level.d, z + i, row, d)
                put(dst, z + i, row, each(lambda p, v: p + v, u, d))

    loop(planes, body, level.group)


def presmooth(level, planes, rows, degree):
    def start(z, n):
        for i in range(n):
            for row in rows:
                d = each(lambda v: v * (1.0 / THETA), get(level.f, z + i, row))
                put(level.d, z + i, row, d)
                put(level.u, z + i, row, d)

    loop(planes(0), start, level.group)
    src, dst = level.u, level.v
    for step, weights in enumerate(chebyshev(degree)[1:], 1):
        sweep(level, src, dst, planes(step), rows, weights)
        src, dst = dst, src
    return src, dst


def postsmooth(level, src, dst, planes, rows, degree, own=None):
    for step, weights in enumerate(chebyshev(degree)):
        final = step == degree - 1
        sweep(level, src, dst, planes(step), own if final and own else rows, weights, final)
        src, dst = dst, src
    return src, dst


def residual_pair(level, src, k, rows, buf):
    for i, row in enumerate(rows):
        parts = []
        for _, dinv, r in scaled_residual(level, src, 2 * k + 1, 2, row):
            ok = dinv[0] > 0.0
            parts.append(jnp.where(ok, r[0], 0.0) / jnp.where(ok, dinv[0], 1.0))
        buf[8 * i : 8 * i + 8, :] = parts[0] + parts[1]


def pair_rows(out_rows, in_rows, out_offset, in_offset, count):
    r, c = iota(out_rows, in_rows, 0) - out_offset, iota(out_rows, in_rows, 1) - in_offset
    hit = (r >= 0) & (r < count) & ((c == 2 * r) | (c == 2 * r + 1))
    return jnp.where(hit, 1.0, 0.0).astype(F32)


def pair_lanes(in_lanes, out_lanes, in_offset, out_offset, count, weight):
    r, c = iota(in_lanes, out_lanes, 0) - in_offset, iota(in_lanes, out_lanes, 1) - out_offset
    hit = (c >= 0) & (c < count) & ((r == 2 * c) | (r == 2 * c + 1))
    return jnp.where(hit, weight, 0.0).astype(F32)


def interp(fine, coarse):
    own = jnp.right_shift(fine, 1)
    other = own + 2 * (fine - 2 * own) - 1
    return jnp.where(coarse == own, 0.75, 0.0) + jnp.where(coarse == other, 0.25, 0.0)


def pack(entries, limit=LANES):
    where, tile, offset = {}, 0, 0
    for key, n in entries:
        if n <= 0:
            continue
        if offset + n > limit:
            tile, offset = tile + 1, 0
        where[key] = (tile, offset, n)
        offset += n
    return where, tile + 1


def rows_of(entries):
    where, offset = {}, 16
    for key, n in entries:
        if n <= 0:
            continue
        where[key] = (offset, n)
        offset += n
    return where, -(-(offset + 16) // 8) * 8


def before_rows(ref, place, height):
    if place is None:
        return jnp.zeros((height, LANES), F32)
    offset, n = place
    base = offset + n - height
    value = ref[base : base + height, :]
    return jnp.where(iota(height, LANES, 0) >= height - n, value, 0.0)


def after_rows(ref, place, height):
    if place is None:
        return jnp.zeros((height, LANES), F32)
    offset, n = place
    value = ref[offset : offset + height, :]
    return jnp.where(iota(height, LANES, 0) < n, value, 0.0)


HALO = 4
HALO1 = 10
ROW0, ROW1, ROW2 = 16, 24, 8


class Plan:
    def __init__(self, z, y, x):
        self.z, self.y, self.x = z, y, x
        z1 = z // 2
        self.z1, self.y1, self.x1 = z1, y // 2, x // 2
        reach = lambda p, n: n if p < z else max(0, n - (p - z + 1))
        self.a0 = [(("a", p), reach(p, HALO + 1)) for p in range(z + HALO + 1)]
        self.c0 = [(("c", p), reach(p, HALO)) for p in range(z + HALO)]
        self.f0 = [(("f", p), reach(p, HALO)) for p in range(z + HALO)]
        self.u0 = [(("u", p), reach(p, HALO)) for p in range(z + HALO)]
        far = lambda o, j, n: n if o == 0 else max(0, min(n, n + 2 - (z1 - j)))
        sides = [(o, j) for o in (0, 1) for j in range(z1)]
        self.sides = sides
        self.ac1 = [(("ac", o, j), far(o, j, HALO1 + 1)) for o, j in sides]
        self.a1 = [(("a1", o, j), far(o, j, HALO1 + 1)) for o, j in sides]
        self.c1 = [(("c1", o, j), far(o, j, HALO1)) for o, j in sides]
        self.f1 = [(("f1", o, j), far(o, j, HALO1)) for o, j in sides]
        self.fp = [(("fp", j), HALO1) for j in range(z1)]
        self.yrows, self.ycount = rows_of(self.a0 + self.c0 + self.f0 + self.ac1)
        self.yrows2, self.ycount2 = rows_of(self.u0 + self.fp)
        self.x0, t0 = pack(self.a0 + self.c0 + self.f0)
        self.x1m, t1 = pack(self.a1 + self.c1)
        self.xu, tu = pack(self.u0)
        self.xf, tf = pack(self.f1)
        self.e0, self.e1 = y + 16, y // 2 + 32
        self.xcount = t0 * self.e0 + t1 * self.e1
        self.xcount2 = tu * self.e0 + tf * self.e1
        self.xbase1, self.xbase2 = t0 * self.e0, tu * self.e0
        self.tiles = (t0, t1, tu, tf)
        self.r0, self.r1 = y + 32, y // 2 + 48
        self.own0, self.own1 = list(range(ROW0, ROW0 + y, 8)), list(range(ROW1, ROW1 + y // 2, 8))
        self.wide0 = list(range(ROW0 - HALO, ROW0 + y + HALO, 8))
        self.wide1 = list(range(ROW1 - HALO1, ROW1 + y // 2 + HALO1, 8))


def plane_of(plan, key, core, coeff, rhs, shift, zrecv):
    kind, p = key
    own = {"a": coeff, "f": rhs, "c": shift}[kind]
    if p < plan.z:
        return lambda rows: own[p + core * (plan.z - 1 - 2 * p), rows, :]
    base = {"a": 0, "c": HALO + 1, "f": 2 * HALO + 1}[kind]
    return lambda rows: zrecv[base + p - plan.z, rows, :]


def zpack(plan):
    def kernel(coeff, rhs, shift, out, sems):
        core = lax.axis_index("pz")
        copies = []
        for ref, n in ((coeff, HALO + 1), (shift, HALO), (rhs, HALO)):
            for j in range(n):
                p = plan.z - 1 - j
                i = len(copies)
                copies.append(pltpu.make_async_copy(ref.at[p + core * (plan.z - 1 - 2 * p)], out.at[i], sems.at[i]))
        for copy in copies:
            copy.start()
        for copy in copies:
            copy.wait()

    count = 3 * HALO + 1
    return call(kernel, shape(count, plan.y, plan.x), [pltpu.SemaphoreType.DMA((count,))], raw=True)


def restrict_coefficients(plan):
    def kernel(coeff, shift, out):
        core = lax.axis_index("pz")
        ry = twice(pair_rows(plan.y1, plan.y, 0, 0, plan.y1), 1)
        ra = twice(pair_lanes(LANES, LANES, 0, 0, plan.x1, 0.125), 0)
        rc = twice(pair_lanes(LANES, LANES, 0, plan.x1, plan.x1, 0.125), 0)
        for k in range(plan.z1):
            i = 2 * k + core * (plan.z - 2 - 4 * k)
            a = lanes_dot(rows_dot(ry, coeff[i] + coeff[i + 1]), ra)
            c = lanes_dot(rows_dot(ry, shift[i] + shift[i + 1]), rc)
            out[k] = a + c

    return call(kernel, shape(plan.z1, plan.y1, LANES))


def ypack(plan):
    def kernel(coeff, rhs, shift, zrecv, ac, aco, first, second, both):
        core = lax.axis_index("pz")
        up, down = stage_out(both, "py")
        for key, (offset, n) in plan.yrows.items():
            if key[0] == "ac":
                ref = (ac, aco)[key[1]]
                take, height = (lambda rows, ref=ref, j=key[2]: ref[j, rows, :]), plan.y1
            else:
                take, height = plane_of(plan, key, core, coeff, rhs, shift, zrecv), plan.y
            up[offset : offset + n, :] = take(slice(height - n, height))
            down[offset : offset + n, :] = take(slice(0, n))
        first[...], second[...] = both[0], both[1]

    out = shape(plan.ycount, LANES)
    return call(kernel, [out, out], [vmem(2, plan.ycount, LANES)])


def between(lane, first, n):
    return ((lane - first) & (LANES - 1)) < n


def send_lanes(outs, base, extent, tile, items, rows, width):
    start_row = base + tile * extent
    for height, part in rows:
        lane = iota(height, LANES, 1)
        totals = [jnp.zeros((height, LANES), F32)] * 2
        for get_part, first, n, offset in items:
            value = roll(get_part(part), offset - first)
            totals[0] = jnp.where(between(lane, offset, n), value, totals[0])
            totals[1] = jnp.where(between(lane, offset + n - width, n), value, totals[1])
        for out, total in zip(outs, totals):
            out[start_row : start_row + height, :] = total
        start_row += height


def take_lanes(before, after, rows, offset, n, last):
    lane = iota(rows.stop - rows.start, LANES, 1)
    value = jnp.where(between(lane, offset, n), before[rows, :], after[rows, :])
    return roll(value, last + 1 - n - offset)


def stage_out(both, axis):
    odd = lax.axis_index(axis) & 1
    return both.at[odd], both.at[1 - odd]


def stage_in(both, first, second, axis):
    here = lax.axis_index(axis)
    odd, size_ = here & 1, lax.axis_size(axis)
    valid = (here > 0) & (here < size_ - 1)
    both[1 - odd] = first[...]
    both[odd] = jnp.where(valid, second[...], 0.0)
    return both.at[0], both.at[1]


def xpack(plan):
    def kernel(coeff, rhs, shift, zrecv, ac, aco, ya, yb, first, second, seen, both):
        core = lax.axis_index("pz")
        before, after = stage_in(seen, ya, yb, "py")
        outs = stage_out(both, "px")

        def get0(key):
            plane = plane_of(plan, key, core, coeff, rhs, shift, zrecv)
            place = plan.yrows.get(key)
            return lambda part: (
                before_rows(before, place, 8) if part == 0
                else after_rows(after, place, 8) if part == 2
                else plane(slice(0, plan.y))
            )

        def get1(key):
            place = plan.yrows.get(("ac",) + key[1:])
            ref = (ac, aco)[key[1]]
            return lambda part: (
                before_rows(before, place, 16) if part == 0
                else after_rows(after, place, 16) if part == 2
                else ref[key[2]]
            )

        for tile in range(plan.tiles[0]):
            items = [(get0(k), plan.x - n, n, o) for k, (t, o, n) in plan.x0.items() if t == tile]
            send_lanes(outs, 0, plan.e0, tile, items, ((8, 0), (plan.y, 1), (8, 2)), plan.x)
        side = lambda k: plan.x1 if k[0] == "c1" else 0
        for tile in range(plan.tiles[1]):
            items = [(get1(k), side(k) + plan.x1 - n, n, o) for k, (t, o, n) in plan.x1m.items() if t == tile]
            send_lanes(outs, plan.xbase1, plan.e1, tile, items, ((16, 0), (plan.y1, 1), (16, 2)), plan.x1)
        first[...], second[...] = both[0], both[1]

    out = shape(plan.xcount, LANES)
    return call(kernel, [out, out], [vmem(2, plan.ycount, LANES), vmem(2, plan.xcount, LANES)])


def u_plane(plan, p, u, zrecv):
    if p < plan.z:
        return lambda rows: u[p, rows, :]
    base = (p - plan.z) * plan.y
    return lambda rows: zrecv[base + rows.start : base + rows.stop, :]


def ypack2(plan):
    def kernel(u, zrecv, f, first, second, pair, both):
        up, down = stage_out(both, "py")
        for j in range(plan.z1):
            base = HALO * plan.y + j * plan.y1
            pair[j] = f[j] + zrecv[base : base + plan.y1, :]
        for key, (offset, n) in plan.yrows2.items():
            if key[0] == "fp":
                take, height = (lambda rows, j=key[1]: pair[j, rows, :]), plan.y1
            else:
                take, height = u_plane(plan, key[1], u, zrecv), plan.y
            up[offset : offset + n, :] = take(slice(height - n, height))
            down[offset : offset + n, :] = take(slice(0, n))
        first[...], second[...] = both[0], both[1]

    out = shape(plan.ycount2, LANES)
    return call(kernel, [out, out, shape(plan.z1, plan.y1, LANES)], [vmem(2, plan.ycount2, LANES)])


def xpack2(plan):
    def kernel(u, zrecv, pair, ya, yb, first, second, seen, both):
        before, after = stage_in(seen, ya, yb, "py")
        outs = stage_out(both, "px")

        def get0(key):
            place = plan.yrows2.get(key)
            plane = u_plane(plan, key[1], u, zrecv)
            return lambda part: (
                before_rows(before, place, 8) if part == 0
                else after_rows(after, place, 8) if part == 2
                else plane(slice(0, plan.y))
            )

        def get1(key):
            place = plan.yrows2.get(("fp", key[2]))
            return lambda part: (
                before_rows(before, place, 16) if part == 0
                else after_rows(after, place, 16) if part == 2
                else pair[key[2]]
            )

        for tile in range(plan.tiles[2]):
            items = [(get0(k), plan.x - n, n, o) for k, (t, o, n) in plan.xu.items() if t == tile]
            send_lanes(outs, 0, plan.e0, tile, items, ((8, 0), (plan.y, 1), (8, 2)), plan.x)
        for tile in range(plan.tiles[3]):
            items = [(get1(k), k[1] * plan.x1 + plan.x1 - n, n, o) for k, (t, o, n) in plan.xf.items() if t == tile]
            send_lanes(outs, plan.xbase2, plan.e1, tile, items, ((16, 0), (plan.y1, 1), (16, 2)), plan.x1)
        first[...], second[...] = both[0], both[1]

    out = shape(plan.xcount2, LANES)
    return call(kernel, [out, out], [vmem(2, plan.ycount2, LANES), vmem(2, plan.xcount2, LANES)])


def zero(*groups):
    for ref in [ref for group in groups for ref in group]:
        def body(z, n, ref=ref):
            ref[z - 1] = jnp.zeros(ref.shape[1:], F32)
        loop(ref.shape[0], body)


def fill0(plan, dst, p, plane, yplace, before, after, xplace, left, right):
    main, side = dst
    top, own = ROW0 - 8, plan.y
    main[p + 1, top:ROW0, :] = before_rows(before, yplace, 8)
    main[p + 1, ROW0 : ROW0 + own, :] = plane(slice(0, own))
    main[p + 1, ROW0 + own : ROW0 + own + 8, :] = after_rows(after, yplace, 8)
    value = jnp.zeros((plan.e0, LANES), F32)
    if xplace is not None:
        tile, offset, n = xplace
        rows = slice(tile * plan.e0, (tile + 1) * plan.e0)
        value = take_lanes(left, right, rows, offset, n, LANES - 1)
        value = jnp.where(between(iota(plan.e0, LANES, 1), -n, 2 * n), value, 0.0)
    side[p + 1, top : top + plan.e0, :] = value


def level0(plan, level, core, coeff, rhs, shift, zrecv, before, after, left, right):
    zero(level.u, level.v)
    for kind, dst, planes in (("a", level.v, plan.z + HALO + 1), ("c", level.dinv, plan.z + HALO), ("f", level.f, plan.z + HALO)):
        for p in range(planes):
            key = (kind, p)
            plane = plane_of(plan, key, core, coeff, rhs, shift, zrecv)
            fill0(plan, dst, p, plane, plan.yrows.get(key), before, after, plan.x0.get(key), left, right)
    setup(level, 1.0, plan.z + HALO, plan.wide0, level.v)


def level0_scratch(plan):
    return [vmem(plan.z + HALO + 2, plan.r0, LANES)] * 6


def fill1(plan, dst, p, own, own_first, yplace, before, after, xplace, base, left, right):
    tile, offset, n = xplace
    row = ROW1 - 16
    start_row = base + tile * plan.e1
    for height, value in ((16, before_rows(before, yplace, 16)), (plan.y1, own), (16, after_rows(after, yplace, 16))):
        lane = iota(height, LANES, 1)
        halo = take_lanes(left, right, slice(start_row, start_row + height), offset, n, LANES - 1)
        halo = jnp.where(between(lane, -n, n) | between(lane, plan.x1, n), halo, 0.0)
        dst[p + 1, row : row + height, :] = jnp.where(lane < plan.x1, roll(value, -own_first), halo)
        row, start_row = row + height, start_row + height


def down0(plan):
    def kernel(coeff, rhs, shift, zrecv, ya, yb, xa, xb, u_out, f_out, z_out, *rest):
        kept, (seen_y, seen_x, buf), scratch = rest[:10], rest[10:13], rest[13:]
        core = lax.axis_index("pz")
        ends = stage_in(seen_y, ya, yb, "py") + stage_in(seen_x, xa, xb, "px")
        level = Level(kept + scratch, 2)
        level0(plan, level, core, coeff, rhs, shift, zrecv, *ends)
        src, _ = presmooth(level, lambda s: even(plan.z + HALO - s), plan.wide0, DEG)
        main = src[0]

        def keep(z, n):
            u_out[z - 1] = main[z, ROW0 : ROW0 + plan.y, :]

        loop(plan.z, keep)
        for j in range(HALO):
            z_out[j * plan.y : (j + 1) * plan.y, :] = main[plan.z - j, ROW0 : ROW0 + plan.y, :]
        ry = twice(pair_rows(plan.y1, plan.y, 0, 0, plan.y1), 1)
        rx = twice(pair_lanes(LANES, LANES, 0, 0, plan.x1, 0.125), 0)
        ro = twice(pair_lanes(LANES, LANES, 0, plan.x1, plan.x1, 0.125), 0)

        def residual(z, n):
            residual_pair(level, src, z - 1, plan.own0, buf)
            part = rows_dot(ry, buf[...])
            f_out[z - 1] = lanes_dot(part, rx)
            row = HALO * plan.y + (z - 1) * plan.y1
            z_out[pl.ds(pl.multiple_of(row, 8), plan.y1), :] = lanes_dot(part, ro)

        loop(plan.z1, residual)

    outs = [
        shape(plan.z, plan.y, LANES),
        shape(plan.z1, plan.y1, LANES),
        shape(HALO * plan.y + plan.z1 * plan.y1, LANES),
    ]
    outs += [shape(plan.z + HALO + 2, plan.r0, LANES)] * 10
    seen = [vmem(2, plan.ycount, LANES), vmem(2, plan.xcount, LANES)]
    return call(kernel, outs, seen + [vmem(plan.y, LANES)] + level0_scratch(plan))


def down1(plan):
    planes, z2, y2, x2 = 2 * plan.z1, plan.z1 // 2, plan.y1 // 2, plan.x1 // 2

    def kernel(ac, aco, ya, yb, xa, xb, pair, ya2, yb2, xa2, xb2, wx, wy, wz, f, dinv, u_out, message, *scratch):
        seen_y, seen_x, seen_y2, seen_x2, u, d, buf = scratch
        yends, xends = stage_in(seen_y, ya, yb, "py"), stage_in(seen_x, xa, xb, "px")
        yends2, xends2 = stage_in(seen_y2, ya2, yb2, "py"), stage_in(seen_x2, xa2, xb2, "px")
        level = Level((wx, wy, wz, f, dinv, u, u_out, d))
        zero(level.u, level.v)
        for o, j in plan.sides:
            p = j if o == 0 else planes - 1 - j
            own, place = (ac, aco)[o][j], plan.yrows[("ac", o, j)]
            fill1(plan, u_out, p, own, 0, place, *yends, plan.x1m[("a1", o, j)], plan.xbase1, *xends)
            fill1(plan, dinv, p, own, plan.x1, place, *yends, plan.x1m[("c1", o, j)], plan.xbase1, *xends)
            fill1(plan, f, p, pair[j], o * plan.x1, plan.yrows2[("fp", j)], *yends2, plan.xf[("f1", o, j)], plan.xbase2, *xends2)
        setup(level, 0.25, planes, plan.wide1, level.v)
        src, _ = presmooth(level, lambda s: planes, plan.wide1, DEG)
        assert src[0] is u_out
        ry = twice(pair_rows(y2, plan.y1, 0, 0, y2), 1)
        totals = [jnp.zeros((y2, LANES), F32) for _ in range(3)]
        for k in range(z2):
            residual_pair(level, src, k, plan.own1, buf)
            own = rows_dot(ry, ac[2 * k] + ac[2 * k + 1])
            for i, (part, first) in enumerate(((rows_dot(ry, buf[...]), 0), (own, 0), (own, plan.x1))):
                totals[i] += lanes_dot(part, twice(pair_lanes(LANES, LANES, first, k * x2, x2, 0.125), 0))
        for i in range(3):
            message[i * y2 : (i + 1) * y2, :] = totals[i]

    big = (planes + 2, plan.r1, LANES)
    outs = [shape(*big)] * 6 + [shape(3 * y2, LANES)]
    seen = [vmem(2, n, LANES) for n in (plan.ycount, plan.xcount, plan.ycount2, plan.xcount2)]
    return call(kernel, outs, seen + [vmem(*big)] * 2 + [vmem(plan.y1, LANES)])


def prolong(src, tmp, planes, py, px, rows, group=2):
    def body(z, n):
        for i in range(n):
            for out, matrix in zip(tmp, px):
                out[z + i, rows, :] = rows_dot(py, lanes_dot(src[z + i], matrix))

    loop(planes, body, group)


def correct(level, src, dst, tmp, fine_planes, rows):
    def body(k, n):
        for row in rows:
            column = [get(tmp, k + i, row) for i in range(-1, n + 1)]
            for i in range(n):
                own = each(lambda v: 0.75 * v, column[i + 1])
                for z, far in ((2 * (k + i) - 1, column[i]), (2 * (k + i), column[i + 2])):
                    new = each(
                        lambda p, q, m, v: v + jnp.where(m > 0.0, p + 0.25 * q, 0.0),
                        own, far, get(level.dinv, z, row), get(src, z, row),
                    )
                    put(dst, z, row, new)

    loop(fine_planes // 2, body, level.group)


def coarse(plan):
    planes1 = 2 * plan.z1
    z2, y2, x2 = plan.z1 // 2, plan.y1 // 2, plan.x1 // 2
    planes2, rows2, lanes2 = 2 * z2, 3 * y2, 3 * x2
    planes3, rows3, lanes3 = planes2 // 2, rows2 // 2, lanes2 // 2
    h2, h3 = rows2 + 16, rows3 + 16
    wide2, wide3 = list(range(ROW2, ROW2 + rows2, 8)), list(range(ROW2, ROW2 + rows3, 8))
    block = 3 * y2

    def kernel(own, xa, xb, owno, xao, xbo, wx, wy, wz, f, dinv, u_in, e1, *scratch):
        l2, l3, (u1, d1, buf, tmp3, tmp2, seen) = scratch[:8], scratch[8:16], scratch[16:]
        two, three = Level(l2, 1, 4), Level(l3, 1, 4)
        zero(two.u, two.v, [*l3])
        odd = lax.axis_index("py") & 1
        here = lax.axis_index("py")
        parts = ((1 - odd) * 2, 1, odd * 2)
        edge = (here > 0) & (here < lax.axis_size("py") - 1)
        ok = (jnp.where(odd == 1, True, edge), None, jnp.where(odd == 0, True, edge))
        lane = iota(y2, LANES, 1)
        group = [between(lane, x2 * g, x2) for g in range(4)]
        for side, (mid, first, second) in enumerate(((own, xa, xb), (owno, xao, xbo))):
            left, right = stage_in(seen, first, second, "px")
            for i, dst in enumerate((two.f[0], two.v[0], two.dinv[0])):
                for b in range(3):
                    base = pl.multiple_of(parts[b] * block + i * y2, 8)
                    blocks = [ref[pl.ds(base, y2), :] for ref in (left, mid, right)]
                    if ok[b] is not None:
                        blocks = [jnp.where(ok[b], v, 0.0) for v in blocks]
                    turned = []
                    for s in range(4):
                        value = jnp.zeros((y2, LANES), F32)
                        for k in range(z2):
                            if (k + s) % 4 < 3:
                                value = jnp.where(group[k], blocks[(k + s) % 4], value)
                        turned.append(roll(value, x2 * s))
                    for k in range(z2):
                        value = jnp.zeros((y2, LANES), F32)
                        for g in range(3):
                            value = jnp.where(group[g], turned[(g - k) % 4], value)
                        p = k if side == 0 else planes2 - 1 - k
                        dst[p + 1, ROW2 + b * y2 : ROW2 + (b + 1) * y2, :] = value
        ry = twice(pair_rows(h3, rows2, ROW2, 0, rows3), 1)
        rx = twice(pair_lanes(LANES, LANES, 0, 0, lanes3, 0.125), 0)
        for k in range(planes3):
            for src, dst in ((two.v[0], three.v[0]), (two.dinv[0], three.dinv[0])):
                value = src[2 * k + 1, ROW2 : ROW2 + rows2, :] + src[2 * k + 2, ROW2 : ROW2 + rows2, :]
                dst[k + 1] = lanes_dot(rows_dot(ry, value), rx)
        setup(two, 0.25**2, planes2, wide2, two.v)
        src2, dst2 = presmooth(two, lambda s: planes2, wide2, DEG)
        for k in range(planes3):
            residual_pair(two, src2, k, wide2, buf.at[k])
        for k in range(planes3):
            three.f[0][k + 1] = lanes_dot(rows_dot(ry, buf[k]), rx)
        setup(three, 0.25**3, planes3, wide3, three.v)
        src3, _ = presmooth(three, lambda s: planes3, wide3, CDEG)

        zero([tmp3, tmp2])
        px = twice(interp(iota(LANES, LANES, 1), iota(LANES, LANES, 0)), 0)
        py = twice(interp(iota(h2, h3, 0) - ROW2, iota(h2, h3, 1) - ROW2), 1)
        prolong(src3[0], [tmp3], planes3, py, [px], slice(0, h2), 4)
        correct(two, src2, src2, [tmp3], planes2, wide2)
        src2, _ = postsmooth(two, src2, dst2, lambda s: planes2, wide2, DEG)

        lanes = iota(LANES, LANES, 1)
        lanes = jnp.where(lanes < LANES - 2 * x2 + 16, lanes, lanes - LANES) + 2 * x2
        px = twice(interp(lanes, iota(LANES, LANES, 0)), 0)
        py = twice(interp(iota(plan.r1, h2, 0) - ROW1 + 2 * y2, iota(plan.r1, h2, 1) - ROW2), 1)
        one = Level((wx, wy, wz, f, dinv, u1, e1, d1))
        zero(one.u, one.v)
        prolong(src2[0], [tmp2], planes2, py, [px], slice(0, plan.r1), 2)
        correct(one, [u_in], one.v, [tmp2], planes1, plan.wide1)
        src1, _ = postsmooth(one, one.v, one.u, lambda s: even(min(planes1, plan.z1 + 6 - s)), plan.wide1, DEG)
        assert src1[0] is e1

    big1 = (planes1 + 2, plan.r1, LANES)
    scratch = [vmem(planes2 + 2, h2, LANES)] * 8 + [vmem(planes3 + 2, h3, LANES)] * 8 + [vmem(*big1)] * 2
    scratch += [vmem(planes3, rows2, LANES), vmem(planes3 + 2, h2, LANES), vmem(planes2 + 2, plan.r1, LANES)]
    scratch += [vmem(2, 3 * block, LANES)]
    return call(kernel, shape(*big1), scratch)


def up0(plan):
    planes = plan.z + HALO
    few = HALO // 2 + plan.z1 + 1

    def kernel(u_in, zrecv2, ya2, yb2, xa2, xb2, e1, *rest):
        kept, out, (seen_y2, seen_x2, tmp, tmps), scratch = rest[:10], rest[10], rest[11:15], rest[15:]
        core = lax.axis_index("pz")
        ends2 = stage_in(seen_y2, ya2, yb2, "py") + stage_in(seen_x2, xa2, xb2, "px")
        level = Level(kept + scratch, 2)
        zero(level.u, level.v)
        for p in range(planes):
            key = ("u", p)
            plane = u_plane(plan, p, u_in, zrecv2)
            fill0(plan, level.u, p, plane, plan.yrows2.get(key), *ends2[:2], plan.xu.get(key), *ends2[2:])
        tmp[0] = jnp.zeros(tmp.shape[1:], F32)
        tmps[0] = jnp.zeros(tmp.shape[1:], F32)
        first, count = plan.wide0[0], 8 * len(plan.wide0)
        py = twice(interp(iota(count, plan.r1, 0) + first - ROW0, iota(count, plan.r1, 1) - ROW1), 1)
        lane = iota(LANES, LANES, 1)
        coarse_lane = iota(LANES, LANES, 0)
        coarse_lane = jnp.where(coarse_lane < plan.x1 + 16, coarse_lane, coarse_lane - LANES)
        main = twice(interp(lane, coarse_lane), 0)
        side = twice(interp(jnp.where(lane < LANES // 2, lane + LANES, lane - LANES), coarse_lane), 0)
        prolong(e1, [tmp, tmps], few, py, [main, side], slice(first, first + count))
        correct(level, level.u, level.u, [tmp, tmps], planes, plan.wide0)
        src, _ = postsmooth(level, level.u, level.v, lambda s: even(planes - 1 - s), plan.wide0, DEG, plan.own0)
        for p in range(plan.z):
            out[p + core * (plan.z - 1 - 2 * p)] = src[0][p + 1, ROW0 : ROW0 + plan.y, :]

    seen = [vmem(2, n, LANES) for n in (plan.ycount2, plan.xcount2)]
    tmps = [vmem(few + 2, plan.r0, LANES)] * 2
    return call(kernel, shape(plan.z, plan.y, LANES), seen + tmps + level0_scratch(plan))


def swap(value, axis):
    return lax.ppermute(value, axis, [(0, 1), (1, 0)])


def meet(first, second, axis, wrap=False):
    n = lax.axis_size(axis)
    low = [(i, i + 1) for i in range(0, n - 1, 2)]
    high = [(i, (i + 1) % n) for i in range(1, n if wrap else n - 1, 2)]
    both = lambda pairs: pairs + [(j, i) for i, j in pairs]
    return lax.ppermute(first, axis, both(low)), lax.ppermute(second, axis, both(high))


def local(rhs, coeff, shift):
    plan = Plan(*rhs.shape)
    zrecv = swap(zpack(plan)(coeff, rhs, shift), "pz")
    ac = restrict_coefficients(plan)(coeff, shift)
    aco = swap(ac, "pz")
    ends_y = meet(*ypack(plan)(coeff, rhs, shift, zrecv, ac, aco), "py")
    ends_x = meet(*xpack(plan)(coeff, rhs, shift, zrecv, ac, aco, *ends_y), "px", True)
    fine = (coeff, rhs, shift, zrecv, *ends_y, *ends_x)
    u, f, z_out, *kept = down0(plan)(*fine)
    zrecv2 = swap(z_out, "pz")
    first, second, pair = ypack2(plan)(u, zrecv2, f)
    ends_y2 = meet(first, second, "py")
    ends_x2 = meet(*xpack2(plan)(u, zrecv2, pair, *ends_y2), "px", True)
    *one, message = down1(plan)(ac, aco, *ends_y, *ends_x, pair, *ends_y2, *ends_x2)
    first, second = meet(message, message, "py")
    wide = jnp.concatenate([first, message, second])
    blocks = (wide, *meet(wide, wide, "px", True))
    e1 = coarse(plan)(*blocks, *[swap(b, "pz") for b in blocks], *one)
    return up0(plan)(u, zrecv2, *ends_y2, *ends_x2, e1, *kept)


lower_bound = 0.4
upper_bound = 2.0


def extended(array, sides, width):
    for axis, dim in sides:
        peers, length = (lax.axis_size(axis), array.shape[dim])
        up = [(i, (i + 1) % peers) for i in range(peers - 1)]
        down = [(j, i) for i, j in up]
        last = lax.slice_in_dim(array, length - width, length, axis=dim)
        first = lax.slice_in_dim(array, 0, width, axis=dim)
        before = lax.ppermute(last, axis, up)
        after = lax.ppermute(first, axis, down)
        array = jnp.concatenate([before, array, after], axis=dim)
    return array


def neighbour_views(shape):
    result = []
    for axis_index in range(3):
        for offset in (0, 2):
            index_list = [slice(1, 1 + shape[k]) for k in range(3)]
            index_list[axis_index] = slice(offset, offset + shape[axis_index])
            result.append(tuple(index_list))
    return result


def make_level(coeff_pad, shift_field, factor):
    center = coeff_pad[1:-1, 1:-1, 1:-1]
    weights = jnp.zeros_like(center)
    for view in neighbour_views(center.shape):
        weights = weights + 0.5 * (center + coeff_pad[view])
    inverse = 1.0 / (factor * weights + shift_field)
    return (coeff_pad, shift_field, factor, inverse)


def apply_operator(field_pad, level_data):
    coeff_pad, shift_field, factor, inverse = level_data
    center = field_pad[1:-1, 1:-1, 1:-1]
    coeff_center = coeff_pad[1:-1, 1:-1, 1:-1]
    total = jnp.zeros_like(center)
    for view in neighbour_views(center.shape):
        total = total + 0.5 * (coeff_center + coeff_pad[view]) * (center - field_pad[view])
    return factor * total + shift_field * center


def smooth(field, source, level_data, degree, padder):
    inverse = level_data[3]
    theta = 0.5 * (upper_bound + lower_bound)
    delta = 0.5 * (upper_bound - lower_bound)
    sigma = theta / delta
    rho_now = 1.0 / sigma
    if field is None:
        scaled = source * inverse
        update = scaled / theta
        field = update
    else:
        scaled = (source - apply_operator(padder(field), level_data)) * inverse
        update = scaled / theta
        field = field + update
    for sweep_index in range(degree - 1):
        scaled = (source - apply_operator(padder(field), level_data)) * inverse
        rho_next = 1.0 / (2.0 * sigma - rho_now)
        update = rho_next * rho_now * update + 2.0 * rho_next / delta * scaled
        field = field + update
        rho_now = rho_next
    return field


def restrict(field):
    s0, s1, s2 = field.shape
    return field.reshape(s0 // 2, 2, s1 // 2, 2, s2 // 2, 2).mean(axis=(1, 3, 5))


def refine_axis(padded, axis_index):
    count = padded.shape[axis_index] - 2
    center = lax.slice_in_dim(padded, 1, count + 1, axis=axis_index)
    lower = lax.slice_in_dim(padded, 0, count, axis=axis_index)
    upper = lax.slice_in_dim(padded, 2, count + 2, axis=axis_index)
    even_part = 0.75 * center + 0.25 * lower
    odd_part = 0.75 * center + 0.25 * upper
    stacked = jnp.stack([even_part, odd_part], axis=axis_index + 1)
    shape = list(center.shape)
    shape[axis_index] = 2 * count
    return stacked.reshape(shape)


def prolong_all(padded):
    for axis_index in range(3):
        padded = refine_axis(padded, axis_index)
    return padded


def fine_pad(field):
    return extended(field, (("pz", 0), ("py", 1), ("px", 2)), 1)


def face_pad(field):
    return extended(field, (("pz", 0), ("py", 1), ("px", 2)), 1)


def coarse_face_pad(field):
    return extended(field, (("pz", 0), ("py", 1), ("px", 2)), 1)


def general(rhs, coeff, shift):
    coeff_pad_zero = extended(coeff, (("pz", 0), ("py", 1), ("px", 2)), 1)
    level_zero = make_level(coeff_pad_zero, shift, 1.0)
    field = smooth(None, rhs, level_zero, DEG, fine_pad)
    residual = rhs - apply_operator(fine_pad(field), level_zero)
    fields = [field]
    sources = [rhs, restrict(residual)]
    levels_list = [None]
    coeff_now = restrict(coeff)
    shift_now = restrict(shift)
    for depth in range(1, LEVELS):
        coeff_pad = extended(coeff_now, (("pz", 0), ("py", 1), ("px", 2)), 1)
        levels_list.append(make_level(coeff_pad, shift_now, 0.25**depth))
        coeff_now = restrict(coeff_now)
        shift_now = restrict(shift_now)
    for depth in range(1, LEVELS):
        field = smooth(None, sources[depth], levels_list[depth], DEG, face_pad)
        residual = sources[depth] - apply_operator(face_pad(field), levels_list[depth])
        fields.append(field)
        sources.append(restrict(residual))
    coarse_source = sources[LEVELS]
    coarse_pad = extended(coeff_now, (("pz", 0), ("py", 1), ("px", 2)), 1)
    coarse_level = make_level(coarse_pad, shift_now, 0.25**LEVELS)
    coarse_field = smooth(None, coarse_source, coarse_level, CDEG, coarse_face_pad)
    padded = extended(coarse_field, (("pz", 0), ("py", 1), ("px", 2)), 1)
    for depth in range(LEVELS - 1, 0, -1):
        field = fields[depth] + prolong_all(padded)
        field = smooth(field, sources[depth], levels_list[depth], DEG, face_pad)
        padded = extended(field, (("pz", 0), ("py", 1), ("px", 2)), 1)
    field = fields[0] + prolong_all(padded)
    field = smooth(field, rhs, level_zero, DEG, fine_pad)
    return field


def solution(mesh):
    spec = P("pz", "py", "px")
    body = local if mesh.shape["pz"] == 2 else general

    return jax.shard_map(body, mesh=mesh, in_specs=(spec,) * 3, out_specs=spec, check_vma=False)
```
